256 devices in a mesh: seq: 32 (over y_lo, z, core), chan: 8 (over x, y_hi).
Axes of the slice: x: 4, y: 4 (y_hi: 2, y_lo: 2; y = y_hi * 2 + y_lo), z: 8, core: 2. Of those that a mesh axis runs over, the one named last changes fastest.
Arguments:
- tokens: bfloat16 [4096, 4096], P('seq', 'chan'), may hold values from -6 to 6
- w_in: bfloat16 [4096, 3, 2048], P(None, None, 'chan'), may hold values from -0.09375 to 0.09375
- short_taps: float32 [3, 3, 2048], P(None, None, 'chan'), may hold values from -3 to 3
- skip_gain: float32 [2048], P('chan'), may hold values from 0.5 to 1.5
- filters: float32 [128, 4096], P('chan'), may hold values from -4 to 4
- w_out: bfloat16 [2048, 4096], P('chan'), may hold values from -0.125 to 0.125
Outputs:
- mixed: bfloat16 [4096, 4096], P('seq', 'chan')
The draws below stay inside these ranges and needn't reach their ends.
All inputs are finite; a program needn't handle non-finite values.
Results may differ from the reference program's by a relative error of at most 0.015.
Values may be sent and summed in bfloat16 or wider, within the bound.
No kernel may reach another device: no remote copies, remote signals or barrier semaphores. Data moves between devices by JAX's collectives and lax.ppermute only.
A program may use at most 64 MiB of HBM per device.

```python
import jax
import jax.numpy as jnp
from jax import lax

D = 4096
C = 2048
GS = 16
G = 128
TOKENS = 4096
N_CHAN = 8


def draw_filters(key, part):
    keys = jax.random.split(key, 6)
    length = TOKENS
    steps = jnp.arange(length, dtype=jnp.float32)[None, :]
    slow = jax.random.randint(keys[0], (G, 1), 0, 10) < 5
    slow_rate = jnp.exp(jax.random.uniform(keys[1], (G, 1), jnp.float32, jnp.log(0.2 / length), jnp.log(1.0 / length)))
    fast_rate = jnp.exp(jax.random.uniform(keys[2], (G, 1), jnp.float32, jnp.log(1.0 / 50.0), jnp.log(1.0 / 30.0)))
    rate = jnp.where(slow, slow_rate, fast_rate)
    places = jax.random.randint(keys[3], (G, 4), 0, length)
    factors = jax.random.uniform(keys[4], (G, 4), jnp.float32, 0.5, 0.8)
    passed = (steps[:, None, :] >= places[:, :, None].astype(jnp.float32)).astype(jnp.float32)
    losses = jnp.sum(jnp.log(factors)[:, :, None] * passed, axis=1)
    envelope = jnp.exp(-rate * steps + losses)
    envelope = envelope / jnp.sqrt(jnp.sum(envelope * envelope, axis=1, keepdims=True))
    noise = jnp.clip(jax.random.normal(keys[5], (G, length), jnp.float32), -4.0, 4.0)
    return (envelope * noise).astype(jnp.float32)


def steps_of(rng, extent, pieces, least, top_value):
    gain, own = 1.0, jax.random.fold_in(rng, 6)
    for position, shards_of in pieces:
        heights = jnp.exp(jax.random.uniform(jax.random.fold_in(own, position), (shards_of,), jnp.float32, least / len(pieces), top_value / len(pieces)))
        gain = gain * jnp.repeat(heights, extent[position] // shards_of).reshape([-1 if axis == position else 1 for axis in range(len(extent))])
    return gain


def centred(stream_key, extent, deviation, bound, shards=(), kind=jnp.bfloat16):
    drawn = deviation * jax.random.normal(stream_key, extent, jnp.float32)
    if shards:
        drawn = drawn * steps_of(stream_key, extent, shards, -0.22, 0.18)
    return jnp.clip(drawn, -bound, bound).astype(kind)


def setup_inputs(seed: int = 0) -> dict:
    streams_of = jax.random.split(jax.random.key(seed), 7)
    return {
        "tokens": centred(streams_of[0], (TOKENS, D), 1.0, 6.0, ((0, 32), (1, 8))),
        "w_in": centred(streams_of[1], (D, 3, C), D ** -0.5, 0.09375, ((2, 8),)),
        "short_taps": centred(streams_of[2], (3, 3, C), 0.6, 3.0, ((2, 8),), jnp.float32),
        "skip_gain": jnp.clip(0.5 + 1.0 * jax.random.uniform(streams_of[3], (C,), jnp.float32) ** steps_of(streams_of[3], (C,), ((0, 8),), -0.2, 0.2), 0.5, 1.5),
        "filters": draw_filters(jax.random.fold_in(streams_of[6], 71), 0),
        "w_out": centred(streams_of[5], (C, D), C ** -0.5, 0.125, ((0, 8),)),
    }


def add_block(total, pair):
    part = jnp.dot(pair[0], pair[1], preferred_element_type=jnp.float32).astype(jnp.bfloat16)
    part = lax.optimization_barrier(part).astype(jnp.float32)
    return total + part, None


def reference(tokens, w_in, short_taps, skip_gain, filters, w_out):
    proj = jnp.dot(tokens, w_in.reshape(D, 3 * C), preferred_element_type=jnp.float32)
    proj = proj.astype(jnp.bfloat16).reshape(TOKENS, 3, C).astype(jnp.float32)
    padded = jnp.pad(proj, ((2, 0), (0, 0), (0, 0)))
    streams = short_taps[0] * padded[2:2 + TOKENS]
    streams = streams + short_taps[1] * padded[1:1 + TOKENS]
    streams = streams + short_taps[2] * padded[0:TOKENS]
    gated = (streams[:, 1, :] * streams[:, 2, :]).astype(jnp.bfloat16)
    taps = filters.astype(jnp.bfloat16).astype(jnp.float32)
    per_channel = jnp.repeat(taps, GS, axis=0).T
    length = 2 * TOKENS
    gated_wide = gated.astype(jnp.float32)
    spectrum = jnp.fft.rfft(gated_wide, length, axis=0) * jnp.fft.rfft(per_channel, length, axis=0)
    long_out = jnp.fft.irfft(spectrum, length, axis=0)[:TOKENS].astype(jnp.float32)
    long_out = long_out + skip_gain * gated_wide
    mixer = (streams[:, 0, :] * long_out).astype(jnp.bfloat16)
    mixer_blocks = mixer.reshape(TOKENS, N_CHAN, C // N_CHAN).transpose(1, 0, 2)
    weight_blocks = w_out.reshape(N_CHAN, C // N_CHAN, D)
    total, unused = lax.scan(add_block, jnp.zeros((TOKENS, D), jnp.float32), (mixer_blocks, weight_blocks))
    return total.astype(jnp.bfloat16)
```

```python
import jax
import jax.numpy as jnp
from jax import lax
from jax.experimental import pallas as pl
from jax.experimental.pallas import tpu as pltpu
from jax.sharding import Mesh, PartitionSpec as P

SEQ = ("yl", "z", "core")
CHAN = ("x", "yh")


def chan_shift(block, dx, dy):
    nx, ny = lax.axis_size("x"), lax.axis_size("yh")
    pairs = []
    for x in range(nx):
        for y in range(ny):
            pairs.append((x * ny + y, (x + dx) % nx * ny + (y + dy) % ny))
    return lax.ppermute(block, CHAN, pairs)


def lag_kernel(taps_ref, out_ref):
    count, size = taps_ref.shape
    before = jnp.zeros((size, size), jnp.float32)
    for k in range(count):
        row = taps_ref[k : k + 1, :].astype(jnp.bfloat16).astype(jnp.float32)
        here = jnp.broadcast_to(row, (size, size))
        both = jnp.concatenate([before, here], axis=1)
        turned = pltpu.roll(both, 0, 1, stride=1, stride_axis=0)
        out_ref[k * size : (k + 1) * size, :] = turned[:, size:].astype(jnp.bfloat16)
        before = here


def lag_tiles(taps):
    count, size = taps.shape
    return pl.pallas_call(
        lag_kernel,
        out_shape=jax.ShapeDtypeStruct((count * size, size), jnp.bfloat16),
        cost_estimate=pl.CostEstimate(
            flops=count * size * size, bytes_accessed=2 * count * size * size, transcendentals=0
        ),
        name="lag_tiles",
    )(taps)


def mix_kernel(proj_ref, short_ref, gain_ref, lags_ref, out_ref, acc_ref):
    count, kinds, width, size = proj_ref.shape
    rows = count * width
    lane = lax.broadcasted_iota(jnp.int32, (rows, size), 1)

    def spread(v):
        return jnp.broadcast_to(v[None], (count, width, size)).reshape(rows, size)

    def stream(k):
        here = proj_ref[:, k].astype(jnp.float32).reshape(rows, size)
        before = jnp.concatenate([jnp.zeros((width, size), jnp.float32), here[: rows - width]], axis=0)
        total = spread(short_ref[0, k]) * here
        for j in (1, 2):
            moved = jnp.where(lane < j, pltpu.roll(before, j, 1), pltpu.roll(here, j, 1))
            total = total + spread(short_ref[j, k]) * moved
        return total

    gated = (stream(1) * stream(2)).astype(jnp.bfloat16)
    wide = gated.astype(jnp.float32)
    late = jnp.concatenate([jnp.zeros((width, size), jnp.float32), wide[: rows - width]], axis=0)
    pair = jnp.concatenate([gated, late.astype(jnp.bfloat16)], axis=1)
    acc_ref[...] = spread(gain_ref[...]) * wide
    for m in range(count // 2):
        skip = 2 * width * m
        acc_ref[skip:, :] += jnp.dot(
            pair[: rows - skip],
            lags_ref[2 * size * m : 2 * size * (m + 1), :],
            preferred_element_type=jnp.float32,
        )
    mixed = stream(0) * acc_ref[...]
    out_ref[...] = mixed.astype(jnp.bfloat16)


def mix(proj, short, gain, lags):
    count, kinds, width, size = proj.shape
    rows = count * width
    return pl.pallas_call(
        mix_kernel,
        out_shape=jax.ShapeDtypeStruct((rows, size), jnp.bfloat16),
        scratch_shapes=[pltpu.VMEM((rows, size), jnp.float32)],
        cost_estimate=pl.CostEstimate(
            flops=2 * rows * size * size * count, bytes_accessed=2 * count * size * size, transcendentals=0
        ),
        name="mix",
    )(proj, short, gain, lags)


def shards(tokens, w_in, short_taps, skip_gain, filters, w_out):
    rows, feats = tokens.shape
    width, kinds, chan_dev = w_in.shape
    nx, ny = lax.axis_size("x"), lax.axis_size("yh")
    n_seq = lax.axis_size(SEQ)
    me_seq = lax.axis_index(SEQ)
    ix, iy = lax.axis_index("x"), lax.axis_index("yh")
    per = chan_dev // n_seq
    w3 = jnp.transpose(w_in, (1, 0, 2))

    own = me_seq * per
    short = lax.dynamic_slice_in_dim(short_taps, own, per, 2)
    short = jnp.broadcast_to(short[..., None], (3, kinds, per, rows))
    gain = lax.dynamic_slice_in_dim(skip_gain, own, per, 0)
    gain = jnp.broadcast_to(gain[:, None], (per, rows))
    group = chan_dev // filters.shape[0]
    taps = lax.dynamic_slice_in_dim(filters, own // group, 1, 0)
    lags = lag_tiles(taps.reshape(n_seq, rows))

    def term(block, dx, dy):
        source = (ix - dx) % nx * ny + (iy - dy) % ny
        part = lax.dynamic_slice_in_dim(w3, source * feats, feats, 1)
        return jnp.einsum("kfc,tf->kct", part, block, preferred_element_type=jnp.float32)

    across = chan_shift(tokens, 0, 1)
    acc = term(tokens, 0, 0)
    moves = [(d, 0) for d in (1, nx - 1)] + [(d, 0) for d in range(2, nx - 1)]
    for dx, dy in moves:
        acc = acc + term(chan_shift(tokens, dx, 0), dx, 0)
    acc = acc + term(across, 0, 1)
    for dx, dy in moves:
        acc = acc + term(chan_shift(across, dx, 0), dx, 1)
    proj = acc.astype(jnp.bfloat16).reshape(kinds, n_seq, per, rows)
    proj = jnp.transpose(proj, (1, 0, 2, 3)).reshape(n_seq, kinds * per, rows)
    proj = lax.all_to_all(proj, SEQ, 0, 0, tiled=True).reshape(n_seq, kinds, per, rows)
    mixer = mix(proj, short, gain, lags)
    mixer = lax.all_to_all(mixer.reshape(n_seq, per, rows), SEQ, 0, 0, tiled=True)
    mixer = mixer.reshape(chan_dev, rows)
    parts = [
        jnp.einsum("ct,cf->tf", mixer, w_out[:, j * feats : (j + 1) * feats], preferred_element_type=jnp.float32)
        for j in range(nx * ny)
    ]
    parts = jnp.stack([p.astype(jnp.bfloat16) for p in parts])
    parts = lax.all_to_all(parts, CHAN, 0, 0, tiled=True)
    return jnp.sum(parts.astype(jnp.float32), axis=0).astype(jnp.bfloat16)


def solution(mesh):
    fine = Mesh(mesh.devices.reshape(2, 8, 2, 4, 2), SEQ + CHAN)
    placed = (
        P(SEQ, CHAN),
        P(None, None, CHAN),
        P(None, None, CHAN),
        P(CHAN),
        P(CHAN, None),
        P(CHAN, None),
    )
    return jax.shard_map(
        shards, mesh=fine, in_specs=placed, out_specs=P(SEQ, CHAN), check_vma=False
    )
```

```python
import functools

import jax
import jax.numpy as jnp
from jax import lax
from jax.experimental import pallas as pl
from jax.experimental.pallas import tpu as pltpu
from jax.sharding import Mesh, PartitionSpec as P

SEQ = ("yl", "z", "core")
CHAN = ("x", "yh")
SPLIT = (2, 8, 2, 4, 2)
VMEM = pl.BlockSpec(memory_space=pltpu.VMEM)
SMEM = pl.BlockSpec(memory_space=pltpu.SMEM)
MIB = 1 << 20


def chan_shift(block, dx, dy):
    nx, ny = lax.axis_size("x"), lax.axis_size("yh")
    pairs = []
    for x in range(nx):
        for y in range(ny):
            pairs.append((x * ny + y, (x + dx) % nx * ny + (y + dy) % ny))
    return lax.ppermute(block, CHAN, pairs)


def call(body, name, out_shape, args, scalars=0, scratch=(), vmem=16, flops=1, nbytes=1):
    many = isinstance(out_shape, (tuple, list))
    return pl.pallas_call(
        body,
        out_shape=out_shape,
        in_specs=[SMEM] * scalars + [VMEM] * (len(args) - scalars),
        out_specs=[VMEM] * len(out_shape) if many else VMEM,
        scratch_shapes=list(scratch),
        compiler_params=pltpu.CompilerParams(vmem_limit_bytes=vmem * MIB),
        cost_estimate=pl.CostEstimate(flops=flops, bytes_accessed=nbytes, transcendentals=0),
        name=name,
    )(*args)


def prepare_body(own_ref, filters_ref, taps_ref, gain_ref, lags_ref, short_ref, skip_ref):
    own, group = own_ref[0], own_ref[1]
    size = lags_ref.shape[1]
    count = lags_ref.shape[0] // size
    before = jnp.zeros((size, size), jnp.float32)
    line = filters_ref[pl.ds(group, 1), :].astype(jnp.bfloat16).astype(jnp.float32)
    for k in range(count):
        here = jnp.broadcast_to(line[:, k * size : (k + 1) * size], (size, size))
        both = jnp.concatenate([before, here], axis=1)
        turned = pltpu.roll(both, 0, 1, stride=1, stride_axis=0)
        lags_ref[k * size : (k + 1) * size, :] = turned[:, size:].astype(jnp.bfloat16)
        before = here
    per, width = short_ref.shape[2], taps_ref.shape[2]
    lane = lax.broadcasted_iota(jnp.int32, (per, width), 1)
    row = lax.broadcasted_iota(jnp.int32, (per, width), 0)
    mine = lane == own + row

    def spread(v):
        picked = jnp.where(mine, jnp.broadcast_to(v, (per, width)), 0.0)
        return jnp.broadcast_to(jnp.sum(picked, axis=1, keepdims=True), (per, size))

    for j in range(taps_ref.shape[0]):
        for k in range(taps_ref.shape[1]):
            short_ref[j, k] = spread(taps_ref[j, k : k + 1, :])
    skip_ref[...] = spread(gain_ref[...])


def project_body(count, first, last, *refs):
    source, w_ref = refs[0], refs[1]
    blocks = refs[2 : 2 + count]
    before_ref, out_ref = (None if first else refs[2 + count]), refs[-1]
    feats = blocks[0].shape[1]
    for k in range(w_ref.shape[0]):
        total = None if first else before_ref[k]
        for i, block in enumerate(blocks):
            start = pl.multiple_of(source[i] * feats, feats)
            part = jnp.dot(block[...], w_ref[k, pl.ds(start, feats), :], preferred_element_type=jnp.float32)
            total = part if total is None else total + part
        if last:
            turned = total.T
            out_ref[:, k] = turned.reshape(out_ref.shape[0], out_ref.shape[2], out_ref.shape[3]).astype(jnp.bfloat16)
        else:
            out_ref[k] = total


def mix_body(proj_ref, short_ref, gain_ref, lags_ref, out_ref, acc_ref):
    count, kinds, width, size = proj_ref.shape
    rows = count * width
    lane = lax.broadcasted_iota(jnp.int32, (rows, size), 1)

    def spread(v):
        return jnp.broadcast_to(v[None], (count, width, size)).reshape(rows, size)

    def stream(k):
        here = proj_ref[:, k].astype(jnp.float32).reshape(rows, size)
        before = jnp.concatenate([jnp.zeros((width, size), jnp.float32), here[: rows - width]], axis=0)
        total = spread(short_ref[0, k]) * here
        for j in (1, 2):
            moved = jnp.where(lane < j, pltpu.roll(before, j, 1), pltpu.roll(here, j, 1))
            total = total + spread(short_ref[j, k]) * moved
        return total

    gated = (stream(1) * stream(2)).astype(jnp.bfloat16)
    wide = gated.astype(jnp.float32)
    late = jnp.concatenate([jnp.zeros((width, size), jnp.float32), wide[: rows - width]], axis=0)
    pair = jnp.concatenate([gated, late.astype(jnp.bfloat16)], axis=1)
    acc_ref[...] = spread(gain_ref[...]) * wide
    for m in range(count // 2):
        skip = 2 * width * m
        acc_ref[skip:, :] += jnp.dot(
            pair[: rows - skip],
            lags_ref[2 * size * m : 2 * size * (m + 1), :],
            preferred_element_type=jnp.float32,
        )
    mixed = stream(0) * acc_ref[...]
    out_ref[...] = mixed.reshape(count, width, size).astype(jnp.bfloat16)


def output_body(target, mixer_ref, w_ref, *outs):
    channels = mixer_ref.shape[0] * mixer_ref.shape[1]
    mixer = mixer_ref[...].astype(jnp.float32).reshape(channels, mixer_ref.shape[2])
    mixer = mixer.T.astype(jnp.bfloat16)
    feats = outs[0].shape[1]
    for i, out in enumerate(outs):
        start = pl.multiple_of(target[i] * feats, feats)
        part = jnp.dot(mixer, w_ref[:, pl.ds(start, feats)], preferred_element_type=jnp.float32)
        out[...] = part.astype(out.dtype)


def shards(tokens, w_in, short_taps, skip_gain, filters, w_out):
    rows, feats = tokens.shape
    width, kinds, chan_dev = w_in.shape
    nx, ny = lax.axis_size("x"), lax.axis_size("yh")
    n_seq = lax.axis_size(SEQ)
    ix, iy = lax.axis_index("x"), lax.axis_index("yh")
    per = chan_dev // n_seq
    w3 = jnp.transpose(w_in, (1, 0, 2))
    shape, bf, f32 = jax.ShapeDtypeStruct, jnp.bfloat16, jnp.float32

    def chan_of(dx, dy):
        return (ix + dx + nx) % nx * ny + (iy + dy) % ny

    own = lax.axis_index(SEQ) * per
    group = chan_dev // filters.shape[0]
    lags, short, gain = call(
        prepare_body,
        "prepare",
        [
            shape((n_seq * rows, rows), bf),
            shape((short_taps.shape[0], kinds, per, rows), f32),
            shape((per, rows), f32),
        ],
        [jnp.stack([own, own // group]), filters, short_taps, skip_gain[None]],
        scalars=1,
        flops=8 * n_seq * rows * rows,
        nbytes=4 * n_seq * rows * rows,
    )

    steps = [1, nx - 1] + list(range(2, nx - 1))
    across = chan_shift(tokens, 0, 1)
    near = [tokens] + [chan_shift(tokens, d, 0) for d in steps]
    far = [across] + [chan_shift(across, d, 0) for d in steps]
    from_near = jnp.stack([chan_of(-d, 0) for d in [0] + steps])
    from_far = jnp.stack([chan_of(-d, 1) for d in [0] + steps])
    work = dict(flops=2 * rows * width * kinds * chan_dev // 2, nbytes=width * kinds * chan_dev)
    acc = call(
        functools.partial(project_body, nx, True, False),
        "project_near",
        shape((kinds, rows, chan_dev), f32),
        [from_near, w3] + near,
        scalars=1,
        **work,
    )
    proj = call(
        functools.partial(project_body, nx, False, True),
        "project_far",
        shape((n_seq, kinds, per, rows), bf),
        [from_far, w3] + far + [acc],
        scalars=1,
        **work,
    )
    proj = lax.all_to_all(proj, SEQ, 0, 0, tiled=True)
    mixer = call(
        mix_body,
        "mix",
        shape((n_seq, per, rows), bf),
        [proj, short, gain, lags],
        scratch=[pltpu.VMEM((n_seq * per, rows), f32)],
        flops=n_seq * per * n_seq * rows * rows,
        nbytes=4 * n_seq * rows * rows,
    )
    mixer = lax.all_to_all(mixer, SEQ, 0, 0, tiled=True)

    work = dict(flops=rows * chan_dev * width, nbytes=chan_dev * width)
    block, wide = shape((rows, feats), bf), shape((rows, feats), f32)
    to_far = jnp.stack([chan_of(d, 1) for d in steps + [0]])
    to_near = jnp.stack([chan_of(d, 0) for d in steps + [0]])
    sends = call(output_body, "output_far", [block] * (nx - 1) + [wide], [to_far, mixer, w_out], scalars=1, **work)
    partner = sends[-1]
    for d, part in zip(steps, sends):
        partner = partner + chan_shift(part, d, 0).astype(f32)
    partner = chan_shift(partner.astype(bf), 0, 1)
    sends = call(output_body, "output_near", [block] * (nx - 1) + [wide], [to_near, mixer, w_out], scalars=1, **work)
    total = sends[-1]
    for d, part in zip(steps, sends):
        total = total + chan_shift(part, d, 0).astype(f32)
    return (total + partner.astype(f32)).astype(bf)


def solution(mesh):
    fine = Mesh(mesh.devices.reshape(SPLIT), SEQ + CHAN)
    placed = (
        P(SEQ, CHAN),
        P(None, None, CHAN),
        P(None, None, CHAN),
        P(CHAN),
        P(CHAN, None),
        P(CHAN, None),
    )
    return jax.shard_map(
        shards, mesh=fine, in_specs=placed, out_specs=P(SEQ, CHAN), check_vma=False
    )
```

```python
import functools

import jax
import jax.numpy as jnp
from jax import lax
from jax.experimental import pallas as pl
from jax.experimental.pallas import tpu as pltpu
from jax.sharding import Mesh, PartitionSpec as P


SEQ = ("yl", "z", "core")
CHAN = ("x", "yh")
SPLIT = (2, 8, 2, 4, 2)
VMEM = pl.BlockSpec(memory_space=pltpu.VMEM)
SPACE = {"s": pltpu.SMEM, "v": pltpu.VMEM, "a": pl.ANY, "h": pltpu.HBM}
MIB = 1 << 20


def chan_shift(block, dx, dy):
    nx, ny = lax.axis_size("x"), lax.axis_size("yh")
    pairs = []
    for x in range(nx):
        for y in range(ny):
            pairs.append((x * ny + y, (x + dx) % nx * ny + (y + dy) % ny))
    return lax.ppermute(block, CHAN, pairs)


def call(body, out_shape, args, spaces, scratch=(), vmem=16, flops=1, nbytes=1):
    many = isinstance(out_shape, (tuple, list))
    return pl.pallas_call(
        body,
        out_shape=out_shape,
        in_specs=[pl.BlockSpec(memory_space=SPACE[c]) for c in spaces] + [VMEM] * (len(args) - len(spaces)),
        out_specs=[VMEM] * len(out_shape) if many else VMEM,
        scratch_shapes=list(scratch),
        compiler_params=pltpu.CompilerParams(vmem_limit_bytes=vmem * MIB),
        cost_estimate=pl.CostEstimate(flops=flops, bytes_accessed=nbytes, transcendentals=0),
    )(*args)


def prepare_body(own_ref, filters_ref, taps_ref, gain_ref, lags_ref, short_ref, skip_ref):
    own, group = own_ref[0], own_ref[1]
    size = lags_ref.shape[1]
    count = lags_ref.shape[0] // size
    before = jnp.zeros((size, size), jnp.float32)
    line = filters_ref[pl.ds(group, 1), :].astype(jnp.bfloat16).astype(jnp.float32)
    for k in range(count):
        here = jnp.broadcast_to(line[:, k * size : (k + 1) * size], (size, size))
        both = jnp.concatenate([before, here], axis=1)
        turned = pltpu.roll(both, 0, 1, stride=1, stride_axis=0)
        lags_ref[k * size : (k + 1) * size, :] = turned[:, size:].astype(jnp.bfloat16)
        before = here
    per, width = short_ref.shape[2], taps_ref.shape[2]
    lane = lax.broadcasted_iota(jnp.int32, (per, width), 1)
    row = lax.broadcasted_iota(jnp.int32, (per, width), 0)
    mine = lane == own + row

    def spread(v):
        picked = jnp.where(mine, jnp.broadcast_to(v, (per, width)), 0.0)
        return jnp.broadcast_to(jnp.sum(picked, axis=1, keepdims=True), (per, size))

    for j in range(taps_ref.shape[0]):
        for k in range(taps_ref.shape[1]):
            short_ref[j, k] = spread(taps_ref[j, k : k + 1, :])
    skip_ref[...] = spread(gain_ref[...])


def fetch(order, skip, w_hbm, into, sem):
    feats = into.shape[2]
    loads = []
    for i in range(into.shape[0]):
        start = pl.multiple_of(order[skip + i] * feats, feats)
        loads.append(pltpu.make_async_copy(w_hbm.at[:, pl.ds(start, feats)], into.at[i], sem.at[i]))
        loads[-1].start()
    return loads


def project_first_body(order, w_hbm, *refs):
    blocks, (out_ref, next_ref, w_ref, sem, next_sem) = refs[:-5], refs[-5:]
    count = len(blocks)
    loads = fetch(order, 0, w_hbm, w_ref, sem)
    later = fetch(order, count, w_hbm, next_ref, next_sem)
    for i, block in enumerate(blocks):
        loads[i].wait()
        for k in range(w_ref.shape[1]):
            part = jnp.dot(block[...], w_ref[i, k], preferred_element_type=jnp.float32)
            out_ref[k] = part if i == 0 else out_ref[k] + part
    for load in later:
        load.wait()


def project_near_body(skip, order, w_hbm, w_ref, *refs):
    blocks, (before_ref, out_ref, next_ref, next_sem) = refs[:-4], refs[-4:]
    later = fetch(order, skip, w_hbm, next_ref, next_sem)
    for k in range(w_ref.shape[1]):
        total = before_ref[k]
        for i, block in enumerate(blocks):
            total = total + jnp.dot(block[...], w_ref[i, k], preferred_element_type=jnp.float32)
        out_ref[k] = total
    for load in later:
        load.wait()


def project_far_body(w_ref, *refs):
    blocks, (before_ref, out_ref) = refs[:-2], refs[-2:]
    for k in range(w_ref.shape[1]):
        total = before_ref[k]
        for i, block in enumerate(blocks):
            total = total + jnp.dot(block[...], w_ref[i, k], preferred_element_type=jnp.float32)
        turned = total.T.reshape(out_ref.shape[0], out_ref.shape[2], out_ref.shape[3])
        out_ref[:, k] = turned.astype(jnp.bfloat16)


def mix_body(proj_ref, short_ref, gain_ref, lags_ref, out_ref, acc_ref):
    count, _, width, size = proj_ref.shape
    rows = count * width
    lane = lax.broadcasted_iota(jnp.int32, (rows, size), 1)

    def spread(v):
        return jnp.broadcast_to(v[None], (count, width, size)).reshape(rows, size)

    def stream(k):
        here = proj_ref[:, k].astype(jnp.float32).reshape(rows, size)
        before = jnp.concatenate([jnp.zeros((width, size), jnp.float32), here[: rows - width]], axis=0)
        total = spread(short_ref[0, k]) * here
        for j in (1, 2):
            moved = jnp.where(lane < j, pltpu.roll(before, j, 1), pltpu.roll(here, j, 1))
            total = total + spread(short_ref[j, k]) * moved
        return total

    gated = (stream(1) * stream(2)).astype(jnp.bfloat16)
    wide = gated.astype(jnp.float32)
    late = jnp.concatenate([jnp.zeros((width, size), jnp.float32), wide[: rows - width]], axis=0)
    pair = jnp.concatenate([gated, late.astype(jnp.bfloat16)], axis=1)
    acc_ref[...] = spread(gain_ref[...]) * wide
    for m in range(count // 2):
        skip = 2 * width * m
        acc_ref[skip:, :] += jnp.dot(
            pair[: rows - skip],
            lags_ref[2 * size * m : 2 * size * (m + 1), :],
            preferred_element_type=jnp.float32,
        )
    mixed = stream(0) * acc_ref[...]
    out_ref[...] = mixed.reshape(count, width, size).astype(jnp.bfloat16)


def output_body(target, mixer_ref, w_ref, *outs):
    channels = mixer_ref.shape[0] * mixer_ref.shape[1]
    mixer = mixer_ref[...].astype(jnp.float32).reshape(channels, mixer_ref.shape[2])
    mixer = mixer.T.astype(jnp.bfloat16)
    feats = outs[0].shape[1]
    for i, out in enumerate(outs):
        start = pl.multiple_of(target[i] * feats, feats)
        part = jnp.dot(mixer, w_ref[:, pl.ds(start, feats)], preferred_element_type=jnp.float32)
        out[...] = part.astype(out.dtype)


def layer(tokens, w_in, short_taps, skip_gain, filters, w_out):
    rows, feats = tokens.shape
    width, kinds, chan_dev = w_in.shape
    nx, ny = lax.axis_size("x"), lax.axis_size("yh")
    n_seq = lax.axis_size(SEQ)
    ix, iy = lax.axis_index("x"), lax.axis_index("yh")
    per = chan_dev // n_seq
    w3 = jnp.transpose(w_in, (1, 0, 2))
    shape, bf, f32 = jax.ShapeDtypeStruct, jnp.bfloat16, jnp.float32

    def x_of(d):
        return (ix + d + nx) % nx

    own = lax.axis_index(SEQ) * per
    group = chan_dev // filters.shape[0]
    lags, short, gain = call(
        prepare_body,
        [
            shape((n_seq * rows, rows), bf),
            shape((short_taps.shape[0], kinds, per, rows), f32),
            shape((per, rows), f32),
        ],
        [jnp.stack([own, own // group]), filters, short_taps, skip_gain[None]],
        "s",
        flops=8 * n_seq * rows * rows,
        nbytes=4 * n_seq * rows * rows,
    )

    steps = list(range(2, nx - 1)) + [1, nx - 1]
    across = chan_shift(tokens, 0, 1)
    near, far = [], []
    for d in steps:
        near.append(chan_shift(tokens, d, 0))
    for d in steps:
        far.append(chan_shift(across, d, 0))
    at_first = jnp.stack([ix * ny + iy, ix * ny + 1 - iy])
    at_near = jnp.stack([x_of(-d) * ny + iy for d in steps])
    at_far = jnp.stack([x_of(-d) * ny + 1 - iy for d in steps])
    work = dict(flops=2 * rows * width * kinds * chan_dev // 3, nbytes=width * kinds * chan_dev)
    partial = shape((kinds, rows, chan_dev), f32)
    order = jnp.concatenate([at_first, at_near, at_far])
    chunk = (kinds, feats, chan_dev)
    waits = pltpu.SemaphoreType.DMA((len(steps),))
    acc, w_next = call(
        project_first_body,
        [partial, shape((len(steps),) + chunk, bf)],
        [order, w3, tokens, across],
        "sh",
        scratch=[pltpu.VMEM((2,) + chunk, bf), pltpu.SemaphoreType.DMA((2,)), waits],
        vmem=46,
        **work,
    )
    acc, w_next = call(
        functools.partial(project_near_body, 2 + len(steps)),
        [partial, shape((len(steps),) + chunk, bf)],
        [order, w3, w_next] + near + [acc],
        "sh",
        scratch=[waits],
        vmem=46,
        **work,
    )
    proj = call(
        project_far_body, shape((n_seq, kinds, per, rows), bf), [w_next] + far + [acc], "", **work
    )
    proj = lax.all_to_all(proj, SEQ, 0, 0, tiled=True)
    mixer = call(
        mix_body,
        shape((n_seq, per, rows), bf),
        [proj, short, gain, lags],
        "",
        scratch=[pltpu.VMEM((n_seq * per, rows), f32)],
        flops=n_seq * per * n_seq * rows * rows,
        nbytes=4 * n_seq * rows * rows,
    )
    mixer = lax.all_to_all(mixer, SEQ, 0, 0, tiled=True)
    work = dict(flops=rows * chan_dev * width, nbytes=chan_dev * width)
    block, wide = shape((rows, feats), bf), shape((rows, feats), f32)
    to_near = jnp.stack([x_of(d) * ny + iy for d in steps + [0]])
    to_far = jnp.stack([x_of(d) * ny + 1 - iy for d in steps + [0]])
    sends = call(output_body, [block] * (nx - 1) + [wide], [to_far, mixer, w_out], "s", **work)
    partner = sends[-1]
    for d, part in zip(steps, sends):
        partner = partner + chan_shift(part, d, 0).astype(f32)
    partner = chan_shift(partner.astype(bf), 0, 1)
    sends = call(output_body, [block] * (nx - 1) + [wide], [to_near, mixer, w_out], "s", **work)
    total = sends[-1]
    for d, part in zip(steps, sends):
        total = total + chan_shift(part, d, 0).astype(f32)
    return (total + partner.astype(f32)).astype(bf)


def solution(mesh):
    fine = Mesh(mesh.devices.reshape(SPLIT), SEQ + CHAN)
    placed = (
        P(SEQ, CHAN),
        P(None, None, CHAN),
        P(None, None, CHAN),
        P(CHAN),
        P(CHAN, None),
        P(CHAN, None),
    )
    return jax.shard_map(layer, mesh=fine, in_specs=placed, out_specs=P(SEQ, CHAN), check_vma=False)
```

```python
import functools

import jax
import jax.numpy as jnp
from jax import lax
from jax.experimental import pallas as pl
from jax.experimental.pallas import tpu as pltpu
from jax.sharding import Mesh, PartitionSpec as P


SEQ = ("yl", "z", "core")
CHAN = ("x", "yh")
SPLIT = (2, 8, 2, 4, 2)
VMEM = pl.BlockSpec(memory_space=pltpu.VMEM)
SPACE = {"s": pltpu.SMEM, "v": pltpu.VMEM, "a": pl.ANY, "h": pltpu.HBM}
MIB = 1 << 20


def chan_shift(block, dx, dy):
    nx, ny = lax.axis_size("x"), lax.axis_size("yh")
    pairs = []
    for x in range(nx):
        for y in range(ny):
            pairs.append((x * ny + y, (x + dx) % nx * ny + (y + dy) % ny))
    return lax.ppermute(block, CHAN, pairs)


def call(body, out_shape, args, spaces, scratch=(), vmem=16, flops=1, nbytes=1):
    many = isinstance(out_shape, (tuple, list))
    return pl.pallas_call(
        body,
        out_shape=out_shape,
        in_specs=[pl.BlockSpec(memory_space=SPACE[c]) for c in spaces] + [VMEM] * (len(args) - len(spaces)),
        out_specs=[VMEM] * len(out_shape) if many else VMEM,
        scratch_shapes=list(scratch),
        compiler_params=pltpu.CompilerParams(vmem_limit_bytes=vmem * MIB),
        cost_estimate=pl.CostEstimate(flops=flops, bytes_accessed=nbytes, transcendentals=0),
    )(*args)


def lags_body(group_ref, filters_ref, lags_ref):
    group = group_ref[0]
    size = lags_ref.shape[1]
    count = lags_ref.shape[0] // size
    before = jnp.zeros((size, size), jnp.float32)
    line = filters_ref[pl.ds(group, 1), :].astype(jnp.bfloat16).astype(jnp.float32)
    for k in range(count):
        here = jnp.broadcast_to(line[:, k * size : (k + 1) * size], (size, size))
        both = jnp.concatenate([before, here], axis=1)
        turned = pltpu.roll(both, 0, 1, stride=1, stride_axis=0)
        lags_ref[k * size : (k + 1) * size, :] = turned[:, size:].astype(jnp.bfloat16)
        before = here


def spread_body(own_ref, taps_ref, gain_ref, short_ref, skip_ref):
    own, size = own_ref[0], skip_ref.shape[1]
    per, width = short_ref.shape[2], taps_ref.shape[2]
    lane = lax.broadcasted_iota(jnp.int32, (per, width), 1)
    row = lax.broadcasted_iota(jnp.int32, (per, width), 0)
    mine = lane == own + row

    def spread(v):
        picked = jnp.where(mine, jnp.broadcast_to(v, (per, width)), 0.0)
        return jnp.broadcast_to(jnp.sum(picked, axis=1, keepdims=True), (per, size))

    for j in range(taps_ref.shape[0]):
        for k in range(taps_ref.shape[1]):
            short_ref[j, k] = spread(taps_ref[j, k : k + 1, :])
    skip_ref[...] = spread(gain_ref[...])


def project_body(first, last, source, w_ref, *refs):
    blocks = refs[:-1] if first else refs[:-2]
    before_ref, out_ref = (None if first else refs[-2]), refs[-1]
    feats = blocks[0].shape[1]
    for k in range(w_ref.shape[0]):
        total = None if first else before_ref[k]
        for i, block in enumerate(blocks):
            start = pl.multiple_of(source[i] * feats, feats)
            part = jnp.dot(block[...], w_ref[k, pl.ds(start, feats), :], preferred_element_type=jnp.float32)
            total = part if total is None else total + part
        if last:
            turned = total.T.reshape(out_ref.shape[0], out_ref.shape[2], out_ref.shape[3])
            out_ref[:, k] = turned.astype(jnp.bfloat16)
        else:
            out_ref[k] = total


def mix_body(proj_ref, short_ref, gain_ref, lags_ref, out_ref, acc_ref):
    count, _, width, size = proj_ref.shape
    rows = count * width
    lane = lax.broadcasted_iota(jnp.int32, (rows, size), 1)

    def spread(v):
        return jnp.broadcast_to(v[None], (count, width, size)).reshape(rows, size)

    def stream(k):
        here = proj_ref[:, k].astype(jnp.float32).reshape(rows, size)
        before = jnp.concatenate([jnp.zeros((width, size), jnp.float32), here[: rows - width]], axis=0)
        total = spread(short_ref[0, k]) * here
        for j in (1, 2):
            moved = jnp.where(lane < j, pltpu.roll(before, j, 1), pltpu.roll(here, j, 1))
            total = total + spread(short_ref[j, k]) * moved
        return total

    gated = (stream(1) * stream(2)).astype(jnp.bfloat16)
    wide = gated.astype(jnp.float32)
    late = jnp.concatenate([jnp.zeros((width, size), jnp.float32), wide[: rows - width]], axis=0)
    pair = jnp.concatenate([gated, late.astype(jnp.bfloat16)], axis=1)
    acc_ref[...] = spread(gain_ref[...]) * wide
    for m in range(count // 2):
        skip = 2 * width * m
        acc_ref[skip:, :] += jnp.dot(
            pair[: rows - skip],
            lags_ref[2 * size * m : 2 * size * (m + 1), :],
            preferred_element_type=jnp.float32,
        )
    mixed = stream(0) * acc_ref[...]
    out_ref[...] = mixed.reshape(count, width, size).astype(jnp.bfloat16)


def output_body(target, mixer_ref, w_ref, *outs):
    channels = mixer_ref.shape[0] * mixer_ref.shape[1]
    mixer = mixer_ref[...].astype(jnp.float32).reshape(channels, mixer_ref.shape[2])
    mixer = mixer.T.astype(jnp.bfloat16)
    feats = outs[0].shape[1]
    for i, out in enumerate(outs):
        start = pl.multiple_of(target[i] * feats, feats)
        part = jnp.dot(mixer, w_ref[:, pl.ds(start, feats)], preferred_element_type=jnp.float32)
        out[...] = part.astype(out.dtype)


def layer(tokens, w_in, short_taps, skip_gain, filters, w_out):
    rows, feats = tokens.shape
    width, kinds, chan_dev = w_in.shape
    nx, ny = lax.axis_size("x"), lax.axis_size("yh")
    n_seq = lax.axis_size(SEQ)
    ix, iy = lax.axis_index("x"), lax.axis_index("yh")
    per = chan_dev // n_seq
    w3 = jnp.transpose(w_in, (1, 0, 2))
    shape, bf, f32 = jax.ShapeDtypeStruct, jnp.bfloat16, jnp.float32

    def x_of(d):
        return (ix + d + nx) % nx

    own = lax.axis_index(SEQ) * per
    group = chan_dev // filters.shape[0]
    short, gain = call(
        spread_body,
        [shape((short_taps.shape[0], kinds, per, rows), f32), shape((per, rows), f32)],
        [own[None], short_taps, skip_gain[None]],
        "s",
        flops=8 << 30,
    )
    lags = call(
        lags_body,
        shape((n_seq * rows, rows), bf),
        [(own // group)[None], filters],
        "s",
        flops=8 * n_seq * rows * rows,
        nbytes=4 * n_seq * rows * rows,
    )

    steps = list(range(2, nx - 1)) + [1, nx - 1]
    across = chan_shift(tokens, 0, 1)
    near, far = [], []
    for d in steps:
        near.append(chan_shift(tokens, d, 0))
    for d in steps:
        far.append(chan_shift(across, d, 0))
    at_first = jnp.stack([ix * ny + iy, ix * ny + 1 - iy])
    at_near = jnp.stack([x_of(-d) * ny + iy for d in steps])
    at_far = jnp.stack([x_of(-d) * ny + 1 - iy for d in steps])
    work = dict(flops=2 * rows * width * kinds * chan_dev // 3, nbytes=width * kinds * chan_dev)
    partial = shape((kinds, rows, chan_dev), f32)
    acc = call(
        functools.partial(project_body, True, False),
        partial,
        [jnp.concatenate([at_first, at_near]), w3, tokens, across] + near,
        "s",
        **work,
    )
    proj = call(
        functools.partial(project_body, False, True),
        shape((n_seq, kinds, per, rows), bf),
        [at_far, w3] + far + [acc],
        "s",
        **work,
    )
    proj = lax.all_to_all(proj, SEQ, 0, 0, tiled=True)
    mixer = call(
        mix_body,
        shape((n_seq, per, rows), bf),
        [proj, short, gain, lags],
        "",
        scratch=[pltpu.VMEM((n_seq * per, rows), f32)],
        flops=n_seq * per * n_seq * rows * rows,
        nbytes=4 * n_seq * rows * rows,
    )
    mixer = lax.all_to_all(mixer, SEQ, 0, 0, tiled=True)
    work = dict(flops=rows * chan_dev * width, nbytes=chan_dev * width)
    block, wide = shape((rows, feats), bf), shape((rows, feats), f32)
    to_near = jnp.stack([x_of(d) * ny + iy for d in steps + [0]])
    to_far = jnp.stack([x_of(d) * ny + 1 - iy for d in steps + [0]])
    sends = call(output_body, [block] * (nx - 1) + [wide], [to_far, mixer, w_out], "s", **work)
    partner = sends[-1]
    for d, part in zip(steps, sends):
        partner = partner + chan_shift(part, d, 0).astype(f32)
    partner = chan_shift(partner.astype(bf), 0, 1)
    sends = call(output_body, [block] * (nx - 1) + [wide], [to_near, mixer, w_out], "s", **work)
    total = sends[-1]
    for d, part in zip(steps, sends):
        total = total + chan_shift(part, d, 0).astype(f32)
    return (total + partner.astype(f32)).astype(bf)


def solution(mesh):
    fine = Mesh(mesh.devices.reshape(SPLIT), SEQ + CHAN)
    placed = (
        P(SEQ, CHAN),
        P(None, None, CHAN),
        P(None, None, CHAN),
        P(CHAN),
        P(CHAN, None),
        P(CHAN, None),
    )
    return jax.shard_map(layer, mesh=fine, in_specs=placed, out_specs=P(SEQ, CHAN), check_vma=False)
```

```python
import jax
import jax.numpy as jnp
from jax import lax
from jax.experimental import pallas as pl
from jax.experimental.pallas import tpu as pltpu
from jax.sharding import Mesh, PartitionSpec as P


SEQ = ("yl", "z", "core")
CHAN = ("x", "yh")
SPLIT = (2, 8, 2, 4, 2)
VMEM = pl.BlockSpec(memory_space=pltpu.VMEM)
SPACE = {"s": pltpu.SMEM, "v": pltpu.VMEM, "a": pl.ANY, "h": pltpu.HBM}
MIB = 1 << 20


def chan_shift(block, dx, dy):
    nx, ny = lax.axis_size("x"), lax.axis_size("yh")
    pairs = []
    for x in range(nx):
        for y in range(ny):
            pairs.append((x * ny + y, (x + dx) % nx * ny + (y + dy) % ny))
    return lax.ppermute(block, CHAN, pairs)


def call(body, out_shape, args, spaces, scratch=(), vmem=16, flops=1, nbytes=1):
    many = isinstance(out_shape, (tuple, list))
    return pl.pallas_call(
        body,
        out_shape=out_shape,
        in_specs=[pl.BlockSpec(memory_space=SPACE[c]) for c in spaces] + [VMEM] * (len(args) - len(spaces)),
        out_specs=[VMEM] * len(out_shape) if many else VMEM,
        scratch_shapes=list(scratch),
        compiler_params=pltpu.CompilerParams(vmem_limit_bytes=vmem * MIB),
        cost_estimate=pl.CostEstimate(flops=flops, bytes_accessed=nbytes, transcendentals=0),
    )(*args)


def lags_body(group_ref, filters_ref, lags_ref):
    group = group_ref[0]
    size = lags_ref.shape[1]
    count = lags_ref.shape[0] // size
    before = jnp.zeros((size, size), jnp.float32)
    line = filters_ref[pl.ds(group, 1), :].astype(jnp.bfloat16).astype(jnp.float32)
    for k in range(count):
        here = jnp.broadcast_to(line[:, k * size : (k + 1) * size], (size, size))
        both = jnp.concatenate([before, here], axis=1)
        turned = pltpu.roll(both, 0, 1, stride=1, stride_axis=0)
        lags_ref[k * size : (k + 1) * size, :] = turned[:, size:].astype(jnp.bfloat16)
        before = here


def spread_body(own_ref, taps_ref, gain_ref, short_ref, skip_ref):
    own, size = own_ref[0], skip_ref.shape[1]
    per, width = short_ref.shape[2], taps_ref.shape[2]
    lane = lax.broadcasted_iota(jnp.int32, (per, width), 1)
    row = lax.broadcasted_iota(jnp.int32, (per, width), 0)
    mine = lane == own + row

    def spread(v):
        picked = jnp.where(mine, jnp.broadcast_to(v, (per, width)), 0.0)
        return jnp.broadcast_to(jnp.sum(picked, axis=1, keepdims=True), (per, size))

    for j in range(taps_ref.shape[0]):
        for k in range(taps_ref.shape[1]):
            short_ref[j, k] = spread(taps_ref[j, k : k + 1, :])
    skip_ref[...] = spread(gain_ref[...])


def fetch(order, skip, w_hbm, into, sem):
    loads = []
    for i in range(into.shape[0]):
        loads.append(pltpu.make_async_copy(w_hbm.at[:, order[skip + i]], into.at[i], sem.at[i]))
        loads[-1].start()
    return loads


def columns_body(other_ref, w_hbm, out_ref, sem):
    parts, feats = out_ref.shape[0], out_ref.shape[2]
    loads = []
    for x in range(parts):
        start = pl.multiple_of((2 * x + other_ref[0]) * feats, feats)
        loads.append(pltpu.make_async_copy(w_hbm.at[:, pl.ds(start, feats)], out_ref.at[x], sem.at[x]))
        loads[-1].start()
    for load in loads:
        load.wait()


def project_near_body(order, w_hbm, *refs):
    blocks, (out_ref, next_ref, w_ref, sem, next_sem) = refs[:-5], refs[-5:]
    count = len(blocks)
    loads = fetch(order, 0, w_hbm, w_ref, sem)
    later = fetch(order, count, w_hbm, next_ref, next_sem)
    for i, block in enumerate(blocks):
        loads[i].wait()
        for k in range(w_ref.shape[1]):
            part = jnp.dot(block[...], w_ref[i, k], preferred_element_type=jnp.float32)
            out_ref[k] = part if i == 0 else out_ref[k] + part
    for load in later:
        load.wait()


def project_far_body(w_ref, *refs):
    blocks, (before_ref, out_ref) = refs[:-2], refs[-2:]
    for k in range(w_ref.shape[1]):
        total = before_ref[k]
        for i, block in enumerate(blocks):
            total = total + jnp.dot(block[...], w_ref[i, k], preferred_element_type=jnp.float32)
        turned = total.T.reshape(out_ref.shape[0], out_ref.shape[2], out_ref.shape[3])
        out_ref[:, k] = turned.astype(jnp.bfloat16)


def mix_body(proj_ref, short_ref, gain_ref, lags_ref, out_ref, acc_ref):
    count, _, width, size = proj_ref.shape
    rows = count * width
    lane = lax.broadcasted_iota(jnp.int32, (rows, size), 1)

    def spread(v):
        return jnp.broadcast_to(v[None], (count, width, size)).reshape(rows, size)

    def stream(k):
        here = proj_ref[:, k].astype(jnp.float32).reshape(rows, size)
        before = jnp.concatenate([jnp.zeros((width, size), jnp.float32), here[: rows - width]], axis=0)
        total = spread(short_ref[0, k]) * here
        for j in (1, 2):
            moved = jnp.where(lane < j, pltpu.roll(before, j, 1), pltpu.roll(here, j, 1))
            total = total + spread(short_ref[j, k]) * moved
        return total

    gated = (stream(1) * stream(2)).astype(jnp.bfloat16)
    wide = gated.astype(jnp.float32)
    late = jnp.concatenate([jnp.zeros((width, size), jnp.float32), wide[: rows - width]], axis=0)
    pair = jnp.concatenate([gated, late.astype(jnp.bfloat16)], axis=1)
    acc_ref[...] = spread(gain_ref[...]) * wide
    for m in range(count // 2):
        skip = 2 * width * m
        acc_ref[skip:, :] += jnp.dot(
            pair[: rows - skip],
            lags_ref[2 * size * m : 2 * size * (m + 1), :],
            preferred_element_type=jnp.float32,
        )
    mixed = (stream(0) * acc_ref[...]).reshape(count, width, size).astype(jnp.bfloat16)
    for y in range(out_ref.shape[1]):
        out_ref[:, y] = mixed


def output_body(index, mixer_ref, w_ref, other_ref, *outs):
    iy = index[0]
    count, ny, per, rows = mixer_ref.shape
    feats = outs[0].shape[1]

    def mixer_of(y):
        mixer = mixer_ref[:, y].astype(jnp.float32).reshape(count * per, rows)
        return mixer.T.astype(jnp.bfloat16)

    mine, others = mixer_of(iy), mixer_of(1 - iy)
    for i, out in enumerate(outs):
        x = index[1 + i]
        start = pl.multiple_of((ny * x + iy) * feats, feats)
        total = jnp.dot(mine, w_ref[:, pl.ds(start, feats)], preferred_element_type=jnp.float32)
        total = total + jnp.dot(others, other_ref[x], preferred_element_type=jnp.float32)
        out[...] = total.astype(out.dtype)


def layer(tokens, w_in, short_taps, skip_gain, filters, w_out):
    rows, feats = tokens.shape
    width, kinds, chan_dev = w_in.shape
    nx, ny = lax.axis_size("x"), lax.axis_size("yh")
    n_seq = lax.axis_size(SEQ)
    ix, iy = lax.axis_index("x"), lax.axis_index("yh")
    per = chan_dev // n_seq
    w3 = jnp.transpose(w_in, (1, 0, 2)).reshape(kinds, nx * ny, feats, chan_dev)
    shape, bf, f32 = jax.ShapeDtypeStruct, jnp.bfloat16, jnp.float32

    def x_of(d):
        return (ix + d + nx) % nx

    own = lax.axis_index(SEQ) * per
    group = chan_dev // filters.shape[0]
    short, gain = call(
        spread_body,
        [shape((short_taps.shape[0], kinds, per, rows), f32), shape((per, rows), f32)],
        [own[None], short_taps, skip_gain[None]],
        "s",
    )
    lags = call(
        lags_body,
        shape((n_seq * rows, rows), bf),
        [(own // group)[None], filters],
        "s",
        flops=8 * n_seq * rows * rows,
        nbytes=4 * n_seq * rows * rows,
    )

    steps = list(range(2, nx - 1)) + [1, nx - 1]
    across = chan_shift(tokens, 0, 1)
    near, far = [], []
    for d in steps:
        near.append(chan_shift(tokens, d, 0))
    for d in steps:
        far.append(chan_shift(across, d, 0))
    at_first = jnp.stack([ix * ny + iy, ix * ny + 1 - iy])
    at_near = jnp.stack([x_of(-d) * ny + iy for d in steps])
    at_far = jnp.stack([x_of(-d) * ny + 1 - iy for d in steps])
    work = dict(flops=2 * rows * width * kinds * chan_dev // 3, nbytes=width * kinds * chan_dev)
    partial = shape((kinds, rows, chan_dev), f32)
    order = jnp.concatenate([at_first, at_near, at_far])
    chunk = (kinds, feats, chan_dev)
    first, dma = 2 + len(steps), pltpu.SemaphoreType.DMA
    columns = call(
        columns_body,
        shape((nx, chan_dev, feats), bf),
        [1 - iy[None], w_out],
        "sh",
        scratch=[dma((nx,))],
        vmem=52,
        nbytes=chan_dev * width,
    )
    acc, w_next = call(
        project_near_body,
        [partial, shape((len(steps),) + chunk, bf)],
        [order, w3, tokens, across] + near,
        "sh",
        scratch=[pltpu.VMEM((first,) + chunk, bf), dma((first,)), dma((len(steps),))],
        vmem=48,
        **work,
    )
    proj = call(
        project_far_body, shape((n_seq, kinds, per, rows), bf), [w_next] + far + [acc], "", **work
    )
    columns = chan_shift(columns, 0, 1)
    proj = lax.all_to_all(proj, SEQ, 0, 0, tiled=True)
    mixer = call(
        mix_body,
        shape((n_seq, ny, per, rows), bf),
        [proj, short, gain, lags],
        "",
        scratch=[pltpu.VMEM((n_seq * per, rows), f32)],
        flops=n_seq * per * n_seq * rows * rows,
        nbytes=4 * n_seq * rows * rows,
    )
    mixer = mixer.reshape(n_seq * ny, per, rows)
    mixer = lax.all_to_all(mixer, SEQ + ("yh",), 0, 0, tiled=True)
    mixer = mixer.reshape(n_seq, ny, per, rows)
    block, wide = shape((rows, feats), bf), shape((rows, feats), f32)
    sends = call(
        output_body,
        [block] * (nx - 1) + [wide],
        [jnp.stack([iy] + [x_of(d) for d in steps + [0]]), mixer, w_out, columns],
        "s",
        flops=2 * rows * chan_dev * width,
        nbytes=2 * chan_dev * width,
    )
    total = sends[-1]
    for d, part in zip(steps, sends):
        total = total + chan_shift(part, d, 0).astype(f32)
    return total.astype(bf)


def solution(mesh):
    fine = Mesh(mesh.devices.reshape(SPLIT), SEQ + CHAN)
    placed = (
        P(SEQ, CHAN),
        P(None, None, CHAN),
        P(None, None, CHAN),
        P(CHAN),
        P(CHAN, None),
        P(CHAN, None),
    )
    return jax.shard_map(layer, mesh=fine, in_specs=placed, out_specs=P(SEQ, CHAN), check_vma=False)
```

```python
import jax
import jax.numpy as jnp
from jax import lax
from jax.experimental import pallas as pl
from jax.experimental.pallas import tpu as pltpu
from jax.sharding import Mesh, PartitionSpec as P


SEQ = ("yl", "z", "core")
CHAN = ("x", "yh")
SPLIT = (2, 8, 2, 4, 2)
VMEM = pl.BlockSpec(memory_space=pltpu.VMEM)
SPACE = {"s": pltpu.SMEM, "v": pltpu.VMEM, "a": pl.ANY, "h": pltpu.HBM}
MIB = 1 << 20


def chan_shift(block, dx, dy):
    nx, ny = lax.axis_size("x"), lax.axis_size("yh")
    pairs = []
    for x in range(nx):
        for y in range(ny):
            pairs.append((x * ny + y, (x + dx) % nx * ny + (y + dy) % ny))
    return lax.ppermute(block, CHAN, pairs)


def call(body, out_shape, args, spaces, scratch=(), vmem=16, flops=1, nbytes=1):
    many = isinstance(out_shape, (tuple, list))
    return pl.pallas_call(
        body,
        out_shape=out_shape,
        in_specs=[pl.BlockSpec(memory_space=SPACE[c]) for c in spaces] + [VMEM] * (len(args) - len(spaces)),
        out_specs=[VMEM] * len(out_shape) if many else VMEM,
        scratch_shapes=list(scratch),
        compiler_params=pltpu.CompilerParams(vmem_limit_bytes=vmem * MIB),
        cost_estimate=pl.CostEstimate(flops=flops, bytes_accessed=nbytes, transcendentals=0),
    )(*args)


def lags_body(group_ref, filters_ref, lags_ref):
    group = group_ref[0]
    size = lags_ref.shape[1]
    count = lags_ref.shape[0] // size
    before = jnp.zeros((size, size), jnp.float32)
    line = filters_ref[pl.ds(group, 1), :].astype(jnp.bfloat16).astype(jnp.float32)
    for k in range(count):
        here = jnp.broadcast_to(line[:, k * size : (k + 1) * size], (size, size))
        both = jnp.concatenate([before, here], axis=1)
        turned = pltpu.roll(both, 0, 1, stride=1, stride_axis=0)
        lags_ref[k * size : (k + 1) * size, :] = turned[:, size:].astype(jnp.bfloat16)
        before = here


def spread_body(own_ref, taps_ref, gain_ref, short_ref, skip_ref):
    own, size = own_ref[0], skip_ref.shape[1]
    per, width = short_ref.shape[2], taps_ref.shape[2]
    lane = lax.broadcasted_iota(jnp.int32, (per, width), 1)
    row = lax.broadcasted_iota(jnp.int32, (per, width), 0)
    mine = lane == own + row

    def spread(v):
        picked = jnp.where(mine, jnp.broadcast_to(v, (per, width)), 0.0)
        return jnp.broadcast_to(jnp.sum(picked, axis=1, keepdims=True), (per, size))

    for j in range(taps_ref.shape[0]):
        for k in range(taps_ref.shape[1]):
            short_ref[j, k] = spread(taps_ref[j, k : k + 1, :])
    skip_ref[...] = spread(gain_ref[...])


def fetch(order, skip, w_hbm, into, sem):
    loads = []
    for i in range(into.shape[0]):
        loads.append(pltpu.make_async_copy(w_hbm.at[:, order[skip + i]], into.at[i], sem.at[i]))
        loads[-1].start()
    return loads


def columns_body(index, w_hbm, out_ref, sem):
    parts, half, feats = out_ref.shape
    rows, loads = pl.ds(pl.multiple_of(index[1] * half, half), half), []
    for x in range(parts):
        start = pl.multiple_of((2 * x + index[0]) * feats, feats)
        loads.append(pltpu.make_async_copy(w_hbm.at[rows, pl.ds(start, feats)], out_ref.at[x], sem.at[x]))
        loads[-1].start()
    for load in loads:
        load.wait()


def project_near_body(order, w_hbm, *refs):
    blocks, (out_ref, next_ref, w_ref, sem, next_sem) = refs[:-5], refs[-5:]
    count = len(blocks)
    loads = fetch(order, 0, w_hbm, w_ref, sem)
    later = fetch(order, count, w_hbm, next_ref, next_sem)
    for i, block in enumerate(blocks):
        loads[i].wait()
        for k in range(w_ref.shape[1]):
            part = jnp.dot(block[...], w_ref[i, k], preferred_element_type=jnp.float32)
            out_ref[k] = part if i == 0 else out_ref[k] + part
    for load in later:
        load.wait()


def project_far_body(w_ref, *refs):
    blocks, (before_ref, out_ref) = refs[:-2], refs[-2:]
    for k in range(w_ref.shape[1]):
        total = before_ref[k]
        for i, block in enumerate(blocks):
            total = total + jnp.dot(block[...], w_ref[i, k], preferred_element_type=jnp.float32)
        turned = total.T.reshape(out_ref.shape[0], out_ref.shape[2], out_ref.shape[3])
        out_ref[:, k] = turned.astype(jnp.bfloat16)


def mix_body(proj_ref, short_ref, gain_ref, lags_ref, out_ref, acc_ref):
    count, _, width, size = proj_ref.shape
    rows = count * width
    lane = lax.broadcasted_iota(jnp.int32, (rows, size), 1)

    def spread(v):
        return jnp.broadcast_to(v[None], (count, width, size)).reshape(rows, size)

    def stream(k):
        here = proj_ref[:, k].astype(jnp.float32).reshape(rows, size)
        before = jnp.concatenate([jnp.zeros((width, size), jnp.float32), here[: rows - width]], axis=0)
        total = spread(short_ref[0, k]) * here
        for j in (1, 2):
            moved = jnp.where(lane < j, pltpu.roll(before, j, 1), pltpu.roll(here, j, 1))
            total = total + spread(short_ref[j, k]) * moved
        return total

    gated = (stream(1) * stream(2)).astype(jnp.bfloat16)
    wide = gated.astype(jnp.float32)
    late = jnp.concatenate([jnp.zeros((width, size), jnp.float32), wide[: rows - width]], axis=0)
    pair = jnp.concatenate([gated, late.astype(jnp.bfloat16)], axis=1)
    acc_ref[...] = spread(gain_ref[...]) * wide
    for m in range(count // 2):
        skip = 2 * width * m
        acc_ref[skip:, :] += jnp.dot(
            pair[: rows - skip],
            lags_ref[2 * size * m : 2 * size * (m + 1), :],
            preferred_element_type=jnp.float32,
        )
    mixed = (stream(0) * acc_ref[...]).reshape(count, width, size).astype(jnp.bfloat16)
    for y in range(out_ref.shape[1]):
        out_ref[:, y] = mixed


def output_body(index, mixer_ref, w_ref, half_ref, twin_ref, *outs):
    iy, core = index[0], index[1]
    count, ny, per, rows = mixer_ref.shape
    half, feats = count // 2, outs[0].shape[1]

    def mixer_of(block):
        block = block.astype(jnp.float32)
        return block.reshape(block.shape[0] * per, rows).T.astype(jnp.bfloat16)

    mine = mixer_of(mixer_ref[:, iy])
    here = mixer_of(mixer_ref[pl.ds(core * half, half), 1 - iy])
    there = mixer_of(mixer_ref[pl.ds((1 - core) * half, half), 1 - iy])
    for i, out in enumerate(outs):
        x = index[2 + i]
        start = pl.multiple_of((ny * x + iy) * feats, feats)
        total = jnp.dot(mine, w_ref[:, pl.ds(start, feats)], preferred_element_type=jnp.float32)
        total = total + jnp.dot(here, half_ref[x], preferred_element_type=jnp.float32)
        total = total + jnp.dot(there, twin_ref[x], preferred_element_type=jnp.float32)
        out[...] = total.astype(out.dtype)


def layer(tokens, w_in, short_taps, skip_gain, filters, w_out):
    rows, feats = tokens.shape
    width, kinds, chan_dev = w_in.shape
    nx, ny = lax.axis_size("x"), lax.axis_size("yh")
    n_seq = lax.axis_size(SEQ)
    ix, iy, core = lax.axis_index("x"), lax.axis_index("yh"), lax.axis_index("core")
    per = chan_dev // n_seq
    w3 = jnp.transpose(w_in, (1, 0, 2)).reshape(kinds, nx * ny, feats, chan_dev)
    shape, bf, f32 = jax.ShapeDtypeStruct, jnp.bfloat16, jnp.float32

    def x_of(d):
        return (ix + d + nx) % nx

    own = lax.axis_index(SEQ) * per
    group = chan_dev // filters.shape[0]
    short, gain = call(
        spread_body,
        [shape((short_taps.shape[0], kinds, per, rows), f32), shape((per, rows), f32)],
        [own[None], short_taps, skip_gain[None]],
        "s",
    )
    lags = call(
        lags_body,
        shape((n_seq * rows, rows), bf),
        [(own // group)[None], filters],
        "s",
        flops=8 * n_seq * rows * rows,
        nbytes=4 * n_seq * rows * rows,
    )

    steps = list(range(2, nx - 1)) + [1, nx - 1]
    across = chan_shift(tokens, 0, 1)
    near, far = [], []
    for d in steps:
        near.append(chan_shift(tokens, d, 0))
    for d in steps:
        far.append(chan_shift(near[0], 0, 1) if d == 2 else chan_shift(across, d, 0))
    at_first = jnp.stack([ix * ny + iy, ix * ny + 1 - iy])
    at_near = jnp.stack([x_of(-d) * ny + iy for d in steps])
    at_far = jnp.stack([x_of(-d) * ny + 1 - iy for d in steps])
    work = dict(flops=2 * rows * width * kinds * chan_dev // 3, nbytes=width * kinds * chan_dev)
    partial = shape((kinds, rows, chan_dev), f32)
    order = jnp.concatenate([at_first, at_near, at_far])
    chunk = (kinds, feats, chan_dev)
    first, dma = 2 + len(steps), pltpu.SemaphoreType.DMA
    columns = call(
        columns_body,
        shape((nx, chan_dev // 2, feats), bf),
        [jnp.stack([1 - iy, core]), w_out],
        "sh",
        scratch=[dma((nx,))],
        vmem=52,
        nbytes=chan_dev * width,
    )
    acc, w_next = call(
        project_near_body,
        [partial, shape((len(steps),) + chunk, bf)],
        [order, w3, tokens, across] + near,
        "sh",
        scratch=[pltpu.VMEM((first,) + chunk, bf), dma((first,)), dma((len(steps),))],
        vmem=48,
        **work,
    )
    proj = call(
        project_far_body, shape((n_seq, kinds, per, rows), bf), [w_next] + far + [acc], "", **work
    )
    columns = chan_shift(columns, 0, 1)
    twin = lax.ppermute(columns, "core", [(0, 1), (1, 0)])
    proj = lax.all_to_all(proj, SEQ, 0, 0, tiled=True)
    mixer = call(
        mix_body,
        shape((n_seq, ny, per, rows), bf),
        [proj, short, gain, lags],
        "",
        scratch=[pltpu.VMEM((n_seq * per, rows), f32)],
        flops=n_seq * per * n_seq * rows * rows,
        nbytes=4 * n_seq * rows * rows,
    )
    mixer = mixer.reshape(n_seq * ny, per, rows)
    mixer = lax.all_to_all(mixer, SEQ + ("yh",), 0, 0, tiled=True)
    mixer = mixer.reshape(n_seq, ny, per, rows)
    block, wide = shape((rows, feats), bf), shape((rows, feats), f32)
    sends = call(
        output_body,
        [block] * (nx - 1) + [wide],
        [jnp.stack([iy, core] + [x_of(d) for d in steps + [0]]), mixer, w_out, columns, twin],
        "s",
        flops=2 * rows * chan_dev * width,
        nbytes=2 * chan_dev * width,
    )
    total = sends[-1]
    for d, part in zip(steps, sends):
        total = total + chan_shift(part, d, 0).astype(f32)
    return total.astype(bf)


def solution(mesh):
    fine = Mesh(mesh.devices.reshape(SPLIT), SEQ + CHAN)
    placed = (
        P(SEQ, CHAN),
        P(None, None, CHAN),
        P(None, None, CHAN),
        P(CHAN),
        P(CHAN, None),
        P(CHAN, None),
    )
    return jax.shard_map(layer, mesh=fine, in_specs=placed, out_specs=P(SEQ, CHAN), check_vma=False)
```

```python
import functools

import jax
import jax.numpy as jnp
from jax import lax
from jax.experimental import pallas as pl
from jax.experimental.pallas import tpu as pltpu
from jax.sharding import Mesh, PartitionSpec as P


SEQ = ("yl", "z", "core")
CHAN = ("x", "yh")
SPLIT = (2, 8, 2, 4, 2)
VMEM = pl.BlockSpec(memory_space=pltpu.VMEM)
SPACE = {"s": pltpu.SMEM, "v": pltpu.VMEM, "a": pl.ANY, "h": pltpu.HBM}
MIB = 1 << 20


def chan_shift(block, dx, dy):
    nx, ny = lax.axis_size("x"), lax.axis_size("yh")
    pairs = []
    for x in range(nx):
        for y in range(ny):
            pairs.append((x * ny + y, (x + dx) % nx * ny + (y + dy) % ny))
    return lax.ppermute(block, CHAN, pairs)


def call(body, out_shape, args, spaces, scratch=(), vmem=16, flops=1, nbytes=1):
    many = isinstance(out_shape, (tuple, list))
    return pl.pallas_call(
        body,
        out_shape=out_shape,
        in_specs=[pl.BlockSpec(memory_space=SPACE[c]) for c in spaces] + [VMEM] * (len(args) - len(spaces)),
        out_specs=[VMEM] * len(out_shape) if many else VMEM,
        scratch_shapes=list(scratch),
        compiler_params=pltpu.CompilerParams(vmem_limit_bytes=vmem * MIB),
        cost_estimate=pl.CostEstimate(flops=flops, bytes_accessed=nbytes, transcendentals=0),
    )(*args)


def lags_body(group_ref, filters_ref, lags_ref):
    group = group_ref[0]
    size = lags_ref.shape[1]
    count = lags_ref.shape[0] // size
    before = jnp.zeros((size, size), jnp.float32)
    line = filters_ref[pl.ds(group, 1), :].astype(jnp.bfloat16).astype(jnp.float32)
    for k in range(count):
        here = jnp.broadcast_to(line[:, k * size : (k + 1) * size], (size, size))
        both = jnp.concatenate([before, here], axis=1)
        turned = pltpu.roll(both, 0, 1, stride=1, stride_axis=0)
        lags_ref[k * size : (k + 1) * size, :] = turned[:, size:].astype(jnp.bfloat16)
        before = here


def spread_body(own_ref, taps_ref, gain_ref, short_ref, skip_ref):
    own, size = own_ref[0], skip_ref.shape[1]
    per, width = short_ref.shape[2], taps_ref.shape[2]
    lane = lax.broadcasted_iota(jnp.int32, (per, width), 1)
    row = lax.broadcasted_iota(jnp.int32, (per, width), 0)
    mine = lane == own + row

    def spread(v):
        picked = jnp.where(mine, jnp.broadcast_to(v, (per, width)), 0.0)
        return jnp.broadcast_to(jnp.sum(picked, axis=1, keepdims=True), (per, size))

    for j in range(taps_ref.shape[0]):
        for k in range(taps_ref.shape[1]):
            short_ref[j, k] = spread(taps_ref[j, k : k + 1, :])
    skip_ref[...] = spread(gain_ref[...])


def fetch(order, skip, w_hbm, into, sem):
    loads = []
    for i in range(into.shape[0]):
        loads.append(pltpu.make_async_copy(w_hbm.at[:, order[skip + i]], into.at[i], sem.at[i]))
        loads[-1].start()
    return loads


def columns_body(index, w_hbm, out_ref, sem):
    parts, count, feats = out_ref.shape
    rows, loads = pl.ds(pl.multiple_of(index[1] * count, count), count), []
    for x in range(parts):
        start = pl.multiple_of((2 * x + index[0]) * feats, feats)
        loads.append(pltpu.make_async_copy(w_hbm.at[rows, pl.ds(start, feats)], out_ref.at[x], sem.at[x]))
        loads[-1].start()
    for load in loads:
        load.wait()


def project_near_body(order, w_hbm, *refs):
    blocks, (out_ref, next_ref, w_ref, sem, next_sem) = refs[:-5], refs[-5:]
    count = len(blocks)
    loads = fetch(order, 0, w_hbm, w_ref, sem)
    later = fetch(order, count, w_hbm, next_ref, next_sem)
    for i, block in enumerate(blocks):
        loads[i].wait()
        for k in range(w_ref.shape[1]):
            part = jnp.dot(block[...], w_ref[i, k], preferred_element_type=jnp.float32)
            out_ref[k] = part if i == 0 else out_ref[k] + part
    for load in later:
        load.wait()


def project_mid_body(skip, w_ref, *refs):
    blocks, (before_ref, out_ref) = refs[:-2], refs[-2:]
    for k in range(w_ref.shape[1]):
        total = before_ref[k]
        for i, block in enumerate(blocks):
            total = total + jnp.dot(block[...], w_ref[skip + i, k], preferred_element_type=jnp.float32)
        out_ref[k] = total


def project_far_body(w_ref, block, before_ref, out_ref):
    for k in range(w_ref.shape[1]):
        total = before_ref[k] + jnp.dot(block[...], w_ref[0, k], preferred_element_type=jnp.float32)
        turned = total.T.reshape(out_ref.shape[0], out_ref.shape[2], out_ref.shape[3])
        out_ref[:, k] = turned.astype(jnp.bfloat16)


def mix_body(proj_ref, short_ref, gain_ref, lags_ref, out_ref, acc_ref):
    count, _, width, size = proj_ref.shape
    rows = count * width
    lane = lax.broadcasted_iota(jnp.int32, (rows, size), 1)

    def spread(v):
        return jnp.broadcast_to(v[None], (count, width, size)).reshape(rows, size)

    def stream(k):
        here = proj_ref[:, k].astype(jnp.float32).reshape(rows, size)
        before = jnp.concatenate([jnp.zeros((width, size), jnp.float32), here[: rows - width]], axis=0)
        total = spread(short_ref[0, k]) * here
        for j in (1, 2):
            moved = jnp.where(lane < j, pltpu.roll(before, j, 1), pltpu.roll(here, j, 1))
            total = total + spread(short_ref[j, k]) * moved
        return total

    gated = (stream(1) * stream(2)).astype(jnp.bfloat16)
    wide = gated.astype(jnp.float32)
    late = jnp.concatenate([jnp.zeros((width, size), jnp.float32), wide[: rows - width]], axis=0)
    pair = jnp.concatenate([gated, late.astype(jnp.bfloat16)], axis=1)
    acc_ref[...] = spread(gain_ref[...]) * wide
    for m in range(count // 2):
        skip = 2 * width * m
        acc_ref[skip:, :] += jnp.dot(
            pair[: rows - skip],
            lags_ref[2 * size * m : 2 * size * (m + 1), :],
            preferred_element_type=jnp.float32,
        )
    mixed = (stream(0) * acc_ref[...]).reshape(count, width, size).astype(jnp.bfloat16)
    for y in range(out_ref.shape[1]):
        out_ref[:, y] = mixed


def output_body(index, half_hbm, twin_hbm, mixer_ref, w_ref, *refs):
    outs, (half_ref, twin_ref, total_ref, sem) = refs[:-4], refs[-4:]
    loads = [
        pltpu.make_async_copy(half_hbm, half_ref, sem.at[0]),
        pltpu.make_async_copy(twin_hbm, twin_ref, sem.at[1]),
    ]
    for load in loads:
        load.start()
    iy, core = index[0], index[1]
    count, _, per, rows = mixer_ref.shape
    half = count // 2

    def mixer_of(block):
        block = block.astype(jnp.float32)
        return block.reshape(block.shape[0] * per, rows).T.astype(jnp.bfloat16)

    mine = mixer_of(mixer_ref[:, iy])
    here = mixer_of(mixer_ref[pl.ds(core * half, half), 1 - iy])
    there = mixer_of(mixer_ref[pl.ds((1 - core) * half, half), 1 - iy])
    for i in range(len(outs)):
        total_ref[i] = jnp.dot(mine, w_ref[index[2 + i]], preferred_element_type=jnp.float32)
    for load in loads:
        load.wait()
    for i, out in enumerate(outs):
        x = index[2 + i]
        total = total_ref[i] + jnp.dot(here, half_ref[x], preferred_element_type=jnp.float32)
        total = total + jnp.dot(there, twin_ref[x], preferred_element_type=jnp.float32)
        out[...] = total.astype(out.dtype)


def layer(tokens, w_in, short_taps, skip_gain, filters, w_out):
    rows, feats = tokens.shape
    width, kinds, chan_dev = w_in.shape
    nx, ny = lax.axis_size("x"), lax.axis_size("yh")
    n_seq = lax.axis_size(SEQ)
    ix, iy, core = lax.axis_index("x"), lax.axis_index("yh"), lax.axis_index("core")
    per = chan_dev // n_seq
    w3 = jnp.transpose(w_in, (1, 0, 2)).reshape(kinds, nx * ny, feats, chan_dev)
    shape, bf, f32 = jax.ShapeDtypeStruct, jnp.bfloat16, jnp.float32

    def x_of(d):
        return (ix + d + nx) % nx

    own = lax.axis_index(SEQ) * per
    group = chan_dev // filters.shape[0]
    short, gain = call(
        spread_body,
        [shape((short_taps.shape[0], kinds, per, rows), f32), shape((per, rows), f32)],
        [own[None], short_taps, skip_gain[None]],
        "s",
    )
    lags = call(
        lags_body,
        shape((n_seq * rows, rows), bf),
        [(own // group)[None], filters],
        "s",
        flops=8 * n_seq * rows * rows,
        nbytes=4 * n_seq * rows * rows,
    )

    steps = list(range(2, nx - 1)) + [1, nx - 1]
    across = chan_shift(tokens, 0, 1)
    near, far = [], []
    for d in steps:
        near.append(chan_shift(tokens, d, 0))
    for d in steps:
        far.append(chan_shift(near[0], 0, 1) if d == 2 else chan_shift(across, d, 0))
    at_near = jnp.stack([x_of(-d) * ny + iy for d in steps])
    at_far = jnp.stack([x_of(-d) * ny + 1 - iy for d in steps])
    work = dict(flops=2 * rows * width * kinds * chan_dev // 3, nbytes=width * kinds * chan_dev)
    partial = shape((kinds, rows, chan_dev), f32)
    order = jnp.concatenate([ix[None] * ny + 1 - iy, at_near, at_far, ix[None] * ny + iy])
    chunk = (kinds, feats, chan_dev)
    first, dma = 1 + len(steps), pltpu.SemaphoreType.DMA
    columns = call(
        columns_body,
        shape((nx, chan_dev // 2, feats), bf),
        [jnp.stack([1 - iy, core]), w_out],
        "sh",
        scratch=[dma((nx,))],
        vmem=52,
        nbytes=chan_dev * width,
    )
    acc, w_next = call(
        project_near_body,
        [partial, shape((first,) + chunk, bf)],
        [order, w3, across] + near,
        "sh",
        scratch=[pltpu.VMEM((first,) + chunk, bf), dma((first,)), dma((first,))],
        vmem=48,
        **work,
    )
    acc = call(functools.partial(project_mid_body, 1), partial, [w_next] + far[1:] + [tokens, acc], "", **work)
    proj = call(project_far_body, shape((n_seq, kinds, per, rows), bf), [w_next, far[0], acc], "", **work)
    columns = lax.ppermute(columns, ("yl", "yh"), [(i, 3 - i) for i in range(4)])
    twin = lax.ppermute(columns, "core", [(0, 1), (1, 0)])
    proj = lax.all_to_all(proj, SEQ, 0, 0, tiled=True)
    mixer = call(
        mix_body,
        shape((n_seq, ny, per, rows), bf),
        [proj, short, gain, lags],
        "",
        scratch=[pltpu.VMEM((n_seq * per, rows), f32)],
        flops=n_seq * per * n_seq * rows * rows,
        nbytes=4 * n_seq * rows * rows,
    )
    mixer = mixer.reshape(n_seq * ny, per, rows)
    mixer = lax.all_to_all(mixer, SEQ + ("yh",), 0, 0, tiled=True)
    mixer = mixer.reshape(n_seq, ny, per, rows)
    own_columns = call(
        columns_body,
        shape((nx, chan_dev, feats), bf),
        [jnp.stack([iy, 0 * iy]), w_out],
        "sh",
        scratch=[dma((nx,))],
        nbytes=chan_dev * width,
    )
    block, wide = shape((rows, feats), bf), shape((rows, feats), f32)
    sends = call(
        output_body,
        [block] * (nx - 1) + [wide],
        [jnp.stack([iy, core] + [x_of(d) for d in steps + [0]]), columns, twin, mixer, own_columns],
        "shh",
        scratch=[
            pltpu.VMEM(columns.shape, bf),
            pltpu.VMEM(columns.shape, bf),
            pltpu.VMEM((nx, rows, feats), f32),
            dma((2,)),
        ],
        flops=2 * rows * chan_dev * width,
        nbytes=2 * chan_dev * width,
    )
    total = sends[-1]
    for d, part in zip(steps, sends):
        total = total + chan_shift(part, d, 0).astype(f32)
    return total.astype(bf)


def solution(mesh):
    fine = Mesh(mesh.devices.reshape(SPLIT), SEQ + CHAN)
    placed = (
        P(SEQ, CHAN),
        P(None, None, CHAN),
        P(None, None, CHAN),
        P(CHAN),
        P(CHAN, None),
        P(CHAN, None),
    )
    return jax.shard_map(layer, mesh=fine, in_specs=placed, out_specs=P(SEQ, CHAN), check_vma=False)
```

```python
import functools

import jax
import jax.numpy as jnp
from jax import lax
from jax.experimental import pallas as pl
from jax.experimental.pallas import tpu as pltpu
from jax.sharding import Mesh, PartitionSpec as P


SEQ = ("yl", "z", "core")
CHAN = ("x", "yh")
SPLIT = (2, 8, 2, 4, 2)
VMEM = pl.BlockSpec(memory_space=pltpu.VMEM)
SPACE = {"s": pltpu.SMEM, "v": pltpu.VMEM, "a": pl.ANY, "h": pltpu.HBM}
MIB = 1 << 20


def chan_shift(block, dx, dy):
    nx, ny = lax.axis_size("x"), lax.axis_size("yh")
    pairs = []
    for x in range(nx):
        for y in range(ny):
            pairs.append((x * ny + y, (x + dx) % nx * ny + (y + dy) % ny))
    return lax.ppermute(block, CHAN, pairs)


def call(body, out_shape, args, spaces, scratch=(), vmem=16, flops=1, nbytes=1):
    many = isinstance(out_shape, (tuple, list))
    return pl.pallas_call(
        body,
        out_shape=out_shape,
        in_specs=[pl.BlockSpec(memory_space=SPACE[c]) for c in spaces] + [VMEM] * (len(args) - len(spaces)),
        out_specs=[VMEM] * len(out_shape) if many else VMEM,
        scratch_shapes=list(scratch),
        compiler_params=pltpu.CompilerParams(vmem_limit_bytes=vmem * MIB),
        cost_estimate=pl.CostEstimate(flops=flops, bytes_accessed=nbytes, transcendentals=0),
    )(*args)


def lags_body(group_ref, filters_ref, lags_ref):
    group = group_ref[0]
    size = lags_ref.shape[1]
    count = lags_ref.shape[0] // size
    before = jnp.zeros((size, size), jnp.float32)
    line = filters_ref[pl.ds(group, 1), :].astype(jnp.bfloat16).astype(jnp.float32)
    for k in range(count):
        here = jnp.broadcast_to(line[:, k * size : (k + 1) * size], (size, size))
        both = jnp.concatenate([before, here], axis=1)
        turned = pltpu.roll(both, 0, 1, stride=1, stride_axis=0)
        lags_ref[k * size : (k + 1) * size, :] = turned[:, size:].astype(jnp.bfloat16)
        before = here


def spread_body(own_ref, taps_ref, gain_ref, short_ref, skip_ref):
    own, size = own_ref[0], skip_ref.shape[1]
    per, width = short_ref.shape[2], taps_ref.shape[2]
    lane = lax.broadcasted_iota(jnp.int32, (per, width), 1)
    row = lax.broadcasted_iota(jnp.int32, (per, width), 0)
    mine = lane == own + row

    def spread(v):
        picked = jnp.where(mine, jnp.broadcast_to(v, (per, width)), 0.0)
        return jnp.broadcast_to(jnp.sum(picked, axis=1, keepdims=True), (per, size))

    for j in range(taps_ref.shape[0]):
        for k in range(taps_ref.shape[1]):
            short_ref[j, k] = spread(taps_ref[j, k : k + 1, :])
    skip_ref[...] = spread(gain_ref[...])


def fetch(order, skip, w_hbm, into, sem):
    loads = []
    for i in range(into.shape[0]):
        loads.append(pltpu.make_async_copy(w_hbm.at[:, order[skip + i]], into.at[i], sem.at[i]))
        loads[-1].start()
    return loads


def columns_body(index, w_hbm, out_ref, sem):
    parts, count, feats = out_ref.shape
    rows, loads = pl.ds(pl.multiple_of(index[1] * count, count), count), []
    for x in range(parts):
        start = pl.multiple_of((2 * x + index[0]) * feats, feats)
        loads.append(pltpu.make_async_copy(w_hbm.at[rows, pl.ds(start, feats)], out_ref.at[x], sem.at[x]))
        loads[-1].start()
    for load in loads:
        load.wait()


def fetch_body(order, w_hbm, out_ref, sem):
    for load in fetch(order, 0, w_hbm, out_ref, sem):
        load.wait()


def project_near_body(order, w_hbm, w_ref, *refs):
    blocks, (out_ref, next_ref, next_sem) = refs[:-3], refs[-3:]
    later = fetch(order, len(blocks), w_hbm, next_ref, next_sem)
    for k in range(w_ref.shape[1]):
        total = jnp.dot(blocks[0][...], w_ref[0, k], preferred_element_type=jnp.float32)
        for i, block in enumerate(blocks[1:]):
            total = total + jnp.dot(block[...], w_ref[1 + i, k], preferred_element_type=jnp.float32)
        out_ref[k] = total
    for load in later:
        load.wait()


def project_mid_body(skip, w_ref, *refs):
    blocks, (before_ref, out_ref) = refs[:-2], refs[-2:]
    for k in range(w_ref.shape[1]):
        total = before_ref[k]
        for i, block in enumerate(blocks):
            total = total + jnp.dot(block[...], w_ref[skip + i, k], preferred_element_type=jnp.float32)
        out_ref[k] = total


def project_far_body(w_ref, *refs):
    blocks, (before_ref, out_ref) = refs[:-2], refs[-2:]
    for k in range(w_ref.shape[1]):
        total = before_ref[k]
        for i, block in enumerate(blocks):
            total = total + jnp.dot(block[...], w_ref[i, k], preferred_element_type=jnp.float32)
        turned = total.T.reshape(out_ref.shape[0], out_ref.shape[2], out_ref.shape[3])
        out_ref[:, k] = turned.astype(jnp.bfloat16)


def mix_body(proj_ref, short_ref, gain_ref, lags_ref, out_ref, acc_ref):
    count, _, width, size = proj_ref.shape
    rows = count * width
    lane = lax.broadcasted_iota(jnp.int32, (rows, size), 1)

    def spread(v):
        return jnp.broadcast_to(v[None], (count, width, size)).reshape(rows, size)

    def stream(k):
        here = proj_ref[:, k].astype(jnp.float32).reshape(rows, size)
        before = jnp.concatenate([jnp.zeros((width, size), jnp.float32), here[: rows - width]], axis=0)
        total = spread(short_ref[0, k]) * here
        for j in (1, 2):
            moved = jnp.where(lane < j, pltpu.roll(before, j, 1), pltpu.roll(here, j, 1))
            total = total + spread(short_ref[j, k]) * moved
        return total

    gated = (stream(1) * stream(2)).astype(jnp.bfloat16)
    wide = gated.astype(jnp.float32)
    late = jnp.concatenate([jnp.zeros((width, size), jnp.float32), wide[: rows - width]], axis=0)
    pair = jnp.concatenate([gated, late.astype(jnp.bfloat16)], axis=1)
    acc_ref[...] = spread(gain_ref[...]) * wide
    for m in range(count // 2):
        skip = 2 * width * m
        acc_ref[skip:, :] += jnp.dot(
            pair[: rows - skip],
            lags_ref[2 * size * m : 2 * size * (m + 1), :],
            preferred_element_type=jnp.float32,
        )
    mixed = (stream(0) * acc_ref[...]).reshape(count, width, size).astype(jnp.bfloat16)
    for y in range(out_ref.shape[1]):
        out_ref[:, y] = mixed


def stack_body(half_hbm, twin_hbm, out_ref, sem):
    half, loads = half_hbm.shape[1], []
    for i, source in enumerate((half_hbm, twin_hbm)):
        loads.append(pltpu.make_async_copy(source, out_ref.at[:, pl.ds(i * half, half)], sem.at[i]))
        loads[-1].start()
    for load in loads:
        load.wait()


def output_body(index, mixer_ref, w_ref, other_ref, *outs):
    iy, core = index[0], index[1]
    count, _, per, rows = mixer_ref.shape
    half = count // 2
    pieces = (
        mixer_ref[:, iy],
        mixer_ref[pl.ds(core * half, half), 1 - iy],
        mixer_ref[pl.ds((1 - core) * half, half), 1 - iy],
    )
    turned = [p.astype(jnp.float32).reshape(p.shape[0] * per, rows).T.astype(jnp.bfloat16) for p in pieces]
    mine, others = turned[0], jnp.concatenate(turned[1:], axis=1)
    for i, out in enumerate(outs):
        x = index[2 + i]
        total = jnp.dot(mine, w_ref[x], preferred_element_type=jnp.float32)
        total = total + jnp.dot(others, other_ref[x], preferred_element_type=jnp.float32)
        out[...] = total.astype(out.dtype)


def layer(tokens, w_in, short_taps, skip_gain, filters, w_out):
    rows, feats = tokens.shape
    width, kinds, chan_dev = w_in.shape
    nx, ny = lax.axis_size("x"), lax.axis_size("yh")
    n_seq = lax.axis_size(SEQ)
    ix, iy, core = lax.axis_index("x"), lax.axis_index("yh"), lax.axis_index("core")
    per = chan_dev // n_seq
    w3 = jnp.transpose(w_in, (1, 0, 2)).reshape(kinds, nx * ny, feats, chan_dev)
    shape, bf, f32 = jax.ShapeDtypeStruct, jnp.bfloat16, jnp.float32

    def x_of(d):
        return (ix + d + nx) % nx

    own = lax.axis_index(SEQ) * per
    group = chan_dev // filters.shape[0]
    short, gain = call(
        spread_body,
        [shape((short_taps.shape[0], kinds, per, rows), f32), shape((per, rows), f32)],
        [own[None], short_taps, skip_gain[None]],
        "s",
    )
    lags = call(
        lags_body,
        shape((n_seq * rows, rows), bf),
        [(own // group)[None], filters],
        "s",
        flops=8 * n_seq * rows * rows,
        nbytes=4 * n_seq * rows * rows,
    )

    steps = list(range(2, nx - 1)) + [1, nx - 1]
    across = chan_shift(tokens, 0, 1)
    near, far = [], []
    for d in steps:
        near.append(chan_shift(tokens, d, 0))
    for d in steps:
        far.append(chan_shift(near[0], 0, 1) if d == 2 else chan_shift(across, d, 0))
    at_near = jnp.stack([x_of(-d) * ny + iy for d in steps])
    at_far = jnp.stack([x_of(-d) * ny + 1 - iy for d in steps])
    work = dict(flops=2 * rows * width * kinds * chan_dev // 3, nbytes=width * kinds * chan_dev)
    partial = shape((kinds, rows, chan_dev), f32)
    order = jnp.concatenate([ix[None] * ny + 1 - iy, at_near, at_far, ix[None] * ny + iy])
    chunk = (kinds, feats, chan_dev)
    first, dma = 1 + len(steps), pltpu.SemaphoreType.DMA
    columns = call(
        columns_body,
        shape((nx, chan_dev // 2, feats), bf),
        [jnp.stack([1 - iy, core]), w_out],
        "sh",
        scratch=[dma((nx,))],
        vmem=52,
        nbytes=chan_dev * width,
    )
    order = jnp.concatenate([order[:first], order[first + 1 : first + 3], order[first : first + 1], order[first + 3 :]])
    w_first = call(
        fetch_body,
        shape((first,) + chunk, bf),
        [order, w3],
        "sh",
        scratch=[dma((first,))],
        vmem=48,
        nbytes=kinds * feats * chan_dev,
    )
    acc, w_next = call(
        project_near_body,
        [partial, shape((first,) + chunk, bf)],
        [order, w3, w_first, across] + near,
        "sh",
        scratch=[dma((first,))],
        vmem=46,
        **work,
    )
    acc = call(functools.partial(project_mid_body, 2), partial, [w_next, far[0], tokens, acc], "", **work)
    proj = call(project_far_body, shape((n_seq, kinds, per, rows), bf), [w_next] + far[1:] + [acc], "", **work)
    columns = lax.ppermute(columns, ("yl", "yh"), [(i, 3 - i) for i in range(4)])
    twin = lax.ppermute(columns, "core", [(0, 1), (1, 0)])
    proj = lax.all_to_all(proj, SEQ, 0, 0, tiled=True)
    mixer = call(
        mix_body,
        shape((n_seq, ny, per, rows), bf),
        [proj, short, gain, lags],
        "",
        scratch=[pltpu.VMEM((n_seq * per, rows), f32)],
        flops=n_seq * per * n_seq * rows * rows,
        nbytes=4 * n_seq * rows * rows,
    )
    mixer = mixer.reshape(n_seq * ny, per, rows)
    mixer = lax.all_to_all(mixer, SEQ + ("yh",), 0, 0, tiled=True)
    mixer = mixer.reshape(n_seq, ny, per, rows)
    own_columns = call(
        columns_body,
        shape((nx, chan_dev, feats), bf),
        [jnp.stack([iy, 0 * iy]), w_out],
        "sh",
        scratch=[dma((nx,))],
        nbytes=chan_dev * width,
    )
    stacked = call(
        stack_body,
        shape((nx, chan_dev, feats), bf),
        [columns, twin],
        "hh",
        scratch=[dma((2,))],
        nbytes=chan_dev * width,
    )
    block, wide = shape((rows, feats), bf), shape((rows, feats), f32)
    sends = call(
        output_body,
        [block] * (nx - 1) + [wide],
        [jnp.stack([iy, core] + [x_of(d) for d in steps + [0]]), mixer, own_columns, stacked],
        "s",
        flops=2 * rows * chan_dev * width,
        nbytes=2 * chan_dev * width,
    )
    total = sends[-1]
    for d, part in zip(steps, sends):
        total = total + chan_shift(part, d, 0).astype(f32)
    return total.astype(bf)


def solution(mesh):
    fine = Mesh(mesh.devices.reshape(SPLIT), SEQ + CHAN)
    placed = (
        P(SEQ, CHAN),
        P(None, None, CHAN),
        P(None, None, CHAN),
        P(CHAN),
        P(CHAN, None),
        P(CHAN, None),
    )
    return jax.shard_map(layer, mesh=fine, in_specs=placed, out_specs=P(SEQ, CHAN), check_vma=False)
```

```python
import functools

import jax
import jax.numpy as jnp
from jax import lax
from jax.experimental import pallas as pl
from jax.experimental.pallas import tpu as pltpu
from jax.sharding import Mesh, PartitionSpec as P


SEQ = ("yl", "z", "core")
CHAN = ("x", "yh")
SPLIT = (2, 8, 2, 4, 2)
VMEM = pl.BlockSpec(memory_space=pltpu.VMEM)
SPACE = {"s": pltpu.SMEM, "v": pltpu.VMEM, "a": pl.ANY, "h": pltpu.HBM}
MIB = 1 << 20


def chan_shift(block, dx, dy):
    nx, ny = lax.axis_size("x"), lax.axis_size("yh")
    pairs = []
    for x in range(nx):
        for y in range(ny):
            pairs.append((x * ny + y, (x + dx) % nx * ny + (y + dy) % ny))
    return lax.ppermute(block, CHAN, pairs)


def call(body, out_shape, args, spaces, scratch=(), vmem=16, flops=1, nbytes=1):
    many = isinstance(out_shape, (tuple, list))
    return pl.pallas_call(
        body,
        out_shape=out_shape,
        in_specs=[pl.BlockSpec(memory_space=SPACE[c]) for c in spaces] + [VMEM] * (len(args) - len(spaces)),
        out_specs=[VMEM] * len(out_shape) if many else VMEM,
        scratch_shapes=list(scratch),
        compiler_params=pltpu.CompilerParams(vmem_limit_bytes=vmem * MIB),
        cost_estimate=pl.CostEstimate(flops=flops, bytes_accessed=nbytes, transcendentals=0),
    )(*args)


def lags_body(group_ref, filters_ref, lags_ref):
    group = group_ref[0]
    size = lags_ref.shape[1]
    count = lags_ref.shape[0] // size
    before = jnp.zeros((size, size), jnp.float32)
    line = filters_ref[pl.ds(group, 1), :].astype(jnp.bfloat16).astype(jnp.float32)
    for k in range(count):
        here = jnp.broadcast_to(line[:, k * size : (k + 1) * size], (size, size))
        both = jnp.concatenate([before, here], axis=1)
        turned = pltpu.roll(both, 0, 1, stride=1, stride_axis=0)
        lags_ref[k * size : (k + 1) * size, :] = turned[:, size:].astype(jnp.bfloat16)
        before = here


def spread_body(own_ref, taps_ref, gain_ref, short_ref, skip_ref):
    own, size = own_ref[0], skip_ref.shape[1]
    per, width = short_ref.shape[2], taps_ref.shape[2]
    lane = lax.broadcasted_iota(jnp.int32, (per, width), 1)
    row = lax.broadcasted_iota(jnp.int32, (per, width), 0)
    mine = lane == own + row

    def spread(v):
        picked = jnp.where(mine, jnp.broadcast_to(v, (per, width)), 0.0)
        return jnp.broadcast_to(jnp.sum(picked, axis=1, keepdims=True), (per, size))

    for j in range(taps_ref.shape[0]):
        for k in range(taps_ref.shape[1]):
            short_ref[j, k] = spread(taps_ref[j, k : k + 1, :])
    skip_ref[...] = spread(gain_ref[...])


def fetch(order, skip, w_hbm, into, sem):
    loads = []
    for i in range(into.shape[0]):
        loads.append(pltpu.make_async_copy(w_hbm.at[:, order[skip + i]], into.at[i], sem.at[i]))
        loads[-1].start()
    return loads


def columns_body(index, w_hbm, out_ref, sem):
    parts, count, feats = out_ref.shape
    rows, loads = pl.ds(pl.multiple_of(index[1] * count, count), count), []
    for x in range(parts):
        start = pl.multiple_of((2 * x + index[0]) * feats, feats)
        loads.append(pltpu.make_async_copy(w_hbm.at[rows, pl.ds(start, feats)], out_ref.at[x], sem.at[x]))
        loads[-1].start()
    for load in loads:
        load.wait()


def project_near_body(order, w_hbm, *refs):
    blocks, (out_ref, next_ref, w_ref, sem, next_sem) = refs[:-5], refs[-5:]
    count = len(blocks)
    loads = fetch(order, 0, w_hbm, w_ref, sem)
    later = fetch(order, count, w_hbm, next_ref, next_sem)
    for i, block in enumerate(blocks):
        loads[i].wait()
        for k in range(w_ref.shape[1]):
            part = jnp.dot(block[...], w_ref[i, k], preferred_element_type=jnp.float32)
            out_ref[k] = part if i == 0 else out_ref[k] + part
    for load in later:
        load.wait()


def project_mid_body(skip, w_ref, *refs):
    blocks, (before_ref, out_ref) = refs[:-2], refs[-2:]
    for k in range(w_ref.shape[1]):
        total = before_ref[k]
        for i, block in enumerate(blocks):
            total = total + jnp.dot(block[...], w_ref[skip + i, k], preferred_element_type=jnp.float32)
        out_ref[k] = total


def project_far_body(w_ref, block, before_ref, out_ref):
    for k in range(w_ref.shape[1]):
        total = before_ref[k] + jnp.dot(block[...], w_ref[0, k], preferred_element_type=jnp.float32)
        turned = total.T.reshape(out_ref.shape[0], out_ref.shape[2], out_ref.shape[3])
        out_ref[:, k] = turned.astype(jnp.bfloat16)


def mix_body(proj_ref, short_ref, gain_ref, lags_ref, out_ref, acc_ref):
    count, _, width, size = proj_ref.shape
    rows = count * width
    lane = lax.broadcasted_iota(jnp.int32, (rows, size), 1)

    def spread(v):
        return jnp.broadcast_to(v[None], (count, width, size)).reshape(rows, size)

    def stream(k):
        here = proj_ref[:, k].astype(jnp.float32).reshape(rows, size)
        before = jnp.concatenate([jnp.zeros((width, size), jnp.float32), here[: rows - width]], axis=0)
        total = spread(short_ref[0, k]) * here
        for j in (1, 2):
            moved = jnp.where(lane < j, pltpu.roll(before, j, 1), pltpu.roll(here, j, 1))
            total = total + spread(short_ref[j, k]) * moved
        return total

    gated = (stream(1) * stream(2)).astype(jnp.bfloat16)
    wide = gated.astype(jnp.float32)
    late = jnp.concatenate([jnp.zeros((width, size), jnp.float32), wide[: rows - width]], axis=0)
    pair = jnp.concatenate([gated, late.astype(jnp.bfloat16)], axis=1)
    acc_ref[...] = spread(gain_ref[...]) * wide
    for m in range(count // 2):
        skip = 2 * width * m
        acc_ref[skip:, :] += jnp.dot(
            pair[: rows - skip],
            lags_ref[2 * size * m : 2 * size * (m + 1), :],
            preferred_element_type=jnp.float32,
        )
    mixed = (stream(0) * acc_ref[...]).reshape(count, width, size).astype(jnp.bfloat16)
    for y in range(out_ref.shape[1]):
        out_ref[:, y] = mixed


def stack_body(half_hbm, twin_hbm, out_ref, sem):
    half, loads = half_hbm.shape[1], []
    for i, source in enumerate((half_hbm, twin_hbm)):
        loads.append(pltpu.make_async_copy(source, out_ref.at[:, pl.ds(i * half, half)], sem.at[i]))
        loads[-1].start()
    for load in loads:
        load.wait()


def output_body(index, mixer_ref, w_ref, other_ref, *outs):
    iy, core = index[0], index[1]
    count, _, per, rows = mixer_ref.shape
    half = count // 2
    pieces = (
        mixer_ref[:, iy],
        mixer_ref[pl.ds(core * half, half), 1 - iy],
        mixer_ref[pl.ds((1 - core) * half, half), 1 - iy],
    )
    turned = [p.astype(jnp.float32).reshape(p.shape[0] * per, rows).T.astype(jnp.bfloat16) for p in pieces]
    mine, others = turned[0], jnp.concatenate(turned[1:], axis=1)
    for i, out in enumerate(outs):
        x = index[2 + i]
        total = jnp.dot(mine, w_ref[x], preferred_element_type=jnp.float32)
        total = total + jnp.dot(others, other_ref[x], preferred_element_type=jnp.float32)
        out[...] = total.astype(out.dtype)


def layer(tokens, w_in, short_taps, skip_gain, filters, w_out):
    rows, feats = tokens.shape
    width, kinds, chan_dev = w_in.shape
    nx, ny = lax.axis_size("x"), lax.axis_size("yh")
    n_seq = lax.axis_size(SEQ)
    ix, iy, core = lax.axis_index("x"), lax.axis_index("yh"), lax.axis_index("core")
    per = chan_dev // n_seq
    w3 = jnp.transpose(w_in, (1, 0, 2)).reshape(kinds, nx * ny, feats, chan_dev)
    shape, bf, f32 = jax.ShapeDtypeStruct, jnp.bfloat16, jnp.float32

    def x_of(d):
        return (ix + d + nx) % nx

    own = lax.axis_index(SEQ) * per
    group = chan_dev // filters.shape[0]
    short, gain = call(
        spread_body,
        [shape((short_taps.shape[0], kinds, per, rows), f32), shape((per, rows), f32)],
        [own[None], short_taps, skip_gain[None]],
        "s",
    )
    lags = call(
        lags_body,
        shape((n_seq * rows, rows), bf),
        [(own // group)[None], filters],
        "s",
        flops=8 * n_seq * rows * rows,
        nbytes=4 * n_seq * rows * rows,
    )

    steps = list(range(2, nx - 1)) + [1, nx - 1]
    across = chan_shift(tokens, 0, 1)
    near, far = [], []
    for d in steps:
        near.append(chan_shift(tokens, d, 0))
    for d in steps:
        far.append(chan_shift(near[0], 0, 1) if d == 2 else chan_shift(across, d, 0))
    at_near = jnp.stack([x_of(-d) * ny + iy for d in steps])
    at_far = jnp.stack([x_of(-d) * ny + 1 - iy for d in steps])
    work = dict(flops=2 * rows * width * kinds * chan_dev // 3, nbytes=width * kinds * chan_dev)
    partial = shape((kinds, rows, chan_dev), f32)
    order = jnp.concatenate([ix[None] * ny + 1 - iy, at_near, at_far, ix[None] * ny + iy])
    chunk = (kinds, feats, chan_dev)
    first, dma = 1 + len(steps), pltpu.SemaphoreType.DMA
    columns = call(
        columns_body,
        shape((nx, chan_dev // 2, feats), bf),
        [jnp.stack([1 - iy, core]), w_out],
        "sh",
        scratch=[dma((nx,))],
        vmem=52,
        nbytes=chan_dev * width,
    )
    acc, w_next = call(
        project_near_body,
        [partial, shape((first,) + chunk, bf)],
        [order, w3, across] + near,
        "sh",
        scratch=[pltpu.VMEM((first,) + chunk, bf), dma((first,)), dma((first,))],
        vmem=48,
        **work,
    )
    acc = call(functools.partial(project_mid_body, 1), partial, [w_next] + far[1:] + [tokens, acc], "", **work)
    proj = call(project_far_body, shape((n_seq, kinds, per, rows), bf), [w_next, far[0], acc], "", **work)
    columns = lax.ppermute(columns, ("yl", "yh"), [(i, 3 - i) for i in range(4)])
    twin = lax.ppermute(columns, "core", [(0, 1), (1, 0)])
    proj = lax.all_to_all(proj, SEQ, 0, 0, tiled=True)
    mixer = call(
        mix_body,
        shape((n_seq, ny, per, rows), bf),
        [proj, short, gain, lags],
        "",
        scratch=[pltpu.VMEM((n_seq * per, rows), f32)],
        flops=n_seq * per * n_seq * rows * rows,
        nbytes=4 * n_seq * rows * rows,
    )
    mixer = mixer.reshape(n_seq * ny, per, rows)
    mixer = lax.all_to_all(mixer, SEQ + ("yh",), 0, 0, tiled=True)
    mixer = mixer.reshape(n_seq, ny, per, rows)
    own_columns = call(
        columns_body,
        shape((nx, chan_dev, feats), bf),
        [jnp.stack([iy, 0 * iy]), w_out],
        "sh",
        scratch=[dma((nx,))],
        nbytes=chan_dev * width,
    )
    stacked = call(
        stack_body,
        shape((nx, chan_dev, feats), bf),
        [columns, twin],
        "hh",
        scratch=[dma((2,))],
        nbytes=chan_dev * width,
    )
    block, wide = shape((rows, feats), bf), shape((rows, feats), f32)
    sends = call(
        output_body,
        [block] * (nx - 1) + [wide],
        [jnp.stack([iy, core] + [x_of(d) for d in steps + [0]]), mixer, own_columns, stacked],
        "s",
        flops=2 * rows * chan_dev * width,
        nbytes=2 * chan_dev * width,
    )
    total = sends[-1]
    for d, part in zip(steps, sends):
        total = total + chan_shift(part, d, 0).astype(f32)
    return total.astype(bf)


def solution(mesh):
    fine = Mesh(mesh.devices.reshape(SPLIT), SEQ + CHAN)
    placed = (
        P(SEQ, CHAN),
        P(None, None, CHAN),
        P(None, None, CHAN),
        P(CHAN),
        P(CHAN, None),
        P(CHAN, None),
    )
    return jax.shard_map(layer, mesh=fine, in_specs=placed, out_specs=P(SEQ, CHAN), check_vma=False)
```
